256 devices in a mesh: gx: 16 (over z, x_hi), gy: 16 (over x_lo, y, core).
Axes of the slice: x: 4 (x_hi: 2, x_lo: 2; x = x_hi * 2 + x_lo), y: 4, z: 8, core: 2. Of those that a mesh axis runs over, the one named last changes fastest.
Arguments:
- density: float32 [64, 256, 128], P('gx', 'gy'), may hold values from 0.05 to 1
- passive: int32 [64, 256, 128], P('gx', 'gy'), may hold values 0 or 1
- element_load: float32 [24, 16, 64, 32], P(None, 'gx', 'gy'), may hold values from -5 to 5
Outputs:
- physical: float32 [64, 256, 128], P('gx', 'gy')
- coarse_solution: float32 [3, 16, 65, 33], P(None, 'gx')
The draws below stay inside these ranges and needn't reach their ends.
All inputs are finite; a program needn't handle non-finite values. No bound on the sum of `passive` on one device may be relied on, other than what follows from the above.
Results may differ from the reference program's by a relative error of at most 0.0001.
Values sent between devices are 32-bit elements; how exact they have to be, the bound alone decides.
A program may use at most 128 MiB of HBM per device.

```python
import math
import jax
import jax.numpy as jnp
import numpy as np
from jax import lax

NZ = 128
SWEEPS = 6
NX = 64
NY = 256
NX2 = 16
NY2 = 64
NZ2 = 32


def draw_element_load(key, part):
    amp_key = jax.random.fold_in(key, 11)
    sign_key = jax.random.fold_in(key, 12)
    noise_key = jax.random.fold_in(key, 13)
    amplitudes = jax.random.uniform(amp_key, (2, 3), jnp.float32, 1.0, 1.5)
    noise = jnp.clip(0.4 * jax.random.normal(noise_key, (24, NX2, NY2, NZ2), jnp.float32), -2.0, 2.0)
    signs = jnp.where(jax.random.bernoulli(sign_key, 0.5, (2, 3)), 1.0, -1.0).astype(jnp.float32)
    weights = amplitudes * signs
    rows = jnp.arange(24)
    component = rows // 8
    corner = rows % 8
    bit_x = corner // 4
    bit_y = corner // 2 % 2
    place_x = jnp.arange(NX2)
    place_y = jnp.arange(NY2)
    parity_x = (1 - 2 * ((place_x[None, :] + bit_x[:, None]) % 2)).astype(jnp.float32)
    parity_y = (1 - 2 * ((place_y[None, :] + bit_y[:, None]) % 2)).astype(jnp.float32)
    weight_x = weights[0][component]
    weight_y = weights[1][component]
    along_x = weight_x[:, None, None, None] * parity_x[:, :, None, None]
    along_y = weight_y[:, None, None, None] * parity_y[:, None, :, None]
    return (along_x + along_y + noise).astype(jnp.float32)


def plant(drawn, own_key, low, high):
    spot = [jax.random.randint(jax.random.fold_in(own_key, axis), (), 0, length) for axis, length in enumerate(drawn.shape)]
    main_axis = drawn.shape.index(max(drawn.shape))
    beside = spot[:main_axis] + [(spot[main_axis] + 1) % drawn.shape[main_axis]] + spot[main_axis + 1:]
    return drawn.at[tuple(spot)].set(low).at[tuple(beside)].set(high)


def shard_levels(own_key, extent, split, least, high):
    gain, own = 1.0, jax.random.fold_in(own_key, 6)
    for axis_at, parts in split:
        heights = jnp.exp(jax.random.uniform(jax.random.fold_in(own, axis_at), (parts,), jnp.float32, least / len(split), high / len(split)))
        gain = gain * jnp.repeat(heights, extent[axis_at] // parts).reshape([-1 if axis == axis_at else 1 for axis in range(len(extent))])
    return gain


def setup_inputs(seed: int = 0) -> dict:
    keys = jax.random.split(jax.random.key(seed), 4)
    return {
        "density": jnp.clip(0.05 + 0.95 * jax.random.uniform(keys[0], (NX, NY, NZ), jnp.float32) ** shard_levels(keys[0], (NX, NY, NZ), ((0, 16), (1, 16)), -0.2, 0.2), 0.05, 1.0),
        "passive": plant((jax.random.randint(keys[1], (NX, NY, NZ), 0, 8) < 1).astype(jnp.int32), jax.random.fold_in(keys[1], 1), 0, 1),
        "element_load": draw_element_load(jax.random.fold_in(keys[3], 71), 0),
    }


RELAX = 0.6
YOUNG_MIN = 0.001
HIGHEST = lax.Precision.HIGHEST

def corner_bits(corner_id):
    return [corner_id >> 2 & 1, corner_id >> 1 & 1, corner_id & 1]

def stiffness_table():
    poisson = 0.3
    lame_first = poisson / ((1.0 + poisson) * (1.0 - 2.0 * poisson))
    lame_shear = 1.0 / (2.0 * (1.0 + poisson))
    elastic = np.zeros((6, 6))
    elastic[:3, :3] = lame_first
    for dim_index in range(3):
        elastic[dim_index, dim_index] += 2.0 * lame_shear
        elastic[3 + dim_index, 3 + dim_index] = lame_shear
    corners = np.array([corner_bits(corner_id) for corner_id in range(8)])
    gauss_points = [0.5 - 0.5 / math.sqrt(3.0), 0.5 + 0.5 / math.sqrt(3.0)]
    matrix_sum = np.zeros((24, 24))
    for gauss_x in gauss_points:
        for gauss_y in gauss_points:
            for gauss_z in gauss_points:
                location = np.array([gauss_x, gauss_y, gauss_z])
                shape_values = np.where(corners == 1, location, 1.0 - location)
                gradients = np.zeros((8, 3))
                for dim_index in range(3):
                    slope_sign = np.where(corners[:, dim_index] == 1, 1.0, -1.0)
                    others = shape_values[:, (dim_index + 1) % 3] * shape_values[:, (dim_index + 2) % 3]
                    gradients[:, dim_index] = slope_sign * others
                strain = np.zeros((6, 24))
                for dim_index in range(3):
                    strain[dim_index, 8 * dim_index:8 * dim_index + 8] = gradients[:, dim_index]
                for shear_index, (dim_p, dim_q) in enumerate([(0, 1), (1, 2), (0, 2)]):
                    strain[3 + shear_index, 8 * dim_p:8 * dim_p + 8] = gradients[:, dim_q]
                    strain[3 + shear_index, 8 * dim_q:8 * dim_q + 8] = gradients[:, dim_p]
                matrix_sum = matrix_sum + 0.125 * strain.T @ elastic @ strain
    return matrix_sum

def prolong_table():
    matrix_set = np.zeros((8, 24, 24))
    for child_id in range(8):
        child_bits = corner_bits(child_id)
        for fine_node in range(8):
            fine_bits = corner_bits(fine_node)
            for coarse_node in range(8):
                coarse_bits = corner_bits(coarse_node)
                factor = 1.0
                for dim_index in range(3):
                    position = (child_bits[dim_index] + fine_bits[dim_index]) / 2.0
                    factor = factor * (position if coarse_bits[dim_index] == 1 else 1.0 - position)
                for component in range(3):
                    matrix_set[child_id, 8 * component + fine_node, 8 * component + coarse_node] = factor
    return matrix_set

def second_table():
    prolong = prolong_table()
    stiffness = stiffness_table()
    tables = []
    for outer_id in range(8):
        for inner_id in range(8):
            inner = prolong[inner_id].T @ stiffness @ prolong[inner_id]
            tables.append(prolong[outer_id].T @ inner @ prolong[outer_id])
    return np.stack(tables, axis=-1).reshape(576, 64)

def smooth(padded):
    size_x = padded.shape[0] - 2
    size_y = padded.shape[1] - 2
    size_z = padded.shape[2] - 2
    summed = jnp.zeros((size_x, size_y, size_z), padded.dtype)
    for off_x in range(3):
        for off_y in range(3):
            for off_z in range(3):
                steps_sq = (off_x - 1) ** 2 + (off_y - 1) ** 2 + (off_z - 1) ** 2
                if steps_sq == 3:
                    continue
                weight = 1.5 - math.sqrt(steps_sq)
                summed = summed + weight * padded[off_x:off_x + size_x, off_y:off_y + size_y, off_z:off_z + size_z]
    return summed

def element_dofs(node_values):
    size_x = node_values.shape[1] - 1
    size_y = node_values.shape[2] - 1
    size_z = node_values.shape[3] - 1
    pieces = []
    for corner_id in range(8):
        offsets = corner_bits(corner_id)
        pieces.append(node_values[:, offsets[0]:offsets[0] + size_x, offsets[1]:offsets[1] + size_y, offsets[2]:offsets[2] + size_z])
    return jnp.stack(pieces, axis=1).reshape(24, size_x, size_y, size_z)

def scatter_nodes(element_values):
    size_x, size_y, size_z = element_values.shape[1:]
    pieces = element_values.reshape(3, 8, size_x, size_y, size_z)
    summed = None
    for corner_id in range(8):
        offsets = corner_bits(corner_id)
        placed = jnp.pad(pieces[:, corner_id], ((0, 0), (offsets[0], 1 - offsets[0]), (offsets[1], 1 - offsets[1]), (offsets[2], 1 - offsets[2])))
        summed = placed if summed is None else summed + placed
    return summed

def apply_blocks(blocks, node_values):
    local = jnp.einsum('abxyz,bxyz->axyz', blocks, element_dofs(node_values), precision=HIGHEST)
    return scatter_nodes(local)

def reference(density, passive, element_load):
    padded = jnp.pad(density, 1)
    ones_pad = jnp.pad(jnp.ones_like(density), 1)
    filtered = smooth(padded) / smooth(ones_pad)
    physical = jnp.where(passive == 1, jnp.ones_like(filtered), filtered)
    modulus = YOUNG_MIN + (1.0 - YOUNG_MIN) * physical ** 3
    table = jnp.asarray(second_table(), jnp.float32)
    grouped = modulus.reshape(NX2, 2, 2, NY2, 2, 2, NZ2, 2, 2).transpose(1, 4, 7, 2, 5, 8, 0, 3, 6).reshape(64, -1)
    blocks = jnp.dot(table, grouped, precision=HIGHEST).reshape(24, 24, NX2, NY2, NZ2)
    diagonal = scatter_nodes(blocks.reshape(576, NX2, NY2, NZ2)[::25])
    right_side = scatter_nodes(element_load)
    movable = lax.broadcasted_iota(jnp.int32, right_side.shape, 1) < NX2
    zeros = jnp.zeros_like(right_side)
    solution = jnp.where(movable, RELAX * right_side / diagonal, zeros)
    for turn_index in range(SWEEPS - 1):
        updated = solution + RELAX * (right_side - apply_blocks(blocks, solution)) / diagonal
        solution = jnp.where(movable, updated, zeros)
    return (physical, solution[:, :NX2])
```

```python
import math

import jax
import jax.numpy as jnp
import numpy as np
from jax import lax
from jax.experimental import pallas as pl
from jax.experimental.pallas import tpu as pltpu
from jax.sharding import PartitionSpec as P

SWEEPS = 6
RELAX = 0.6
YOUNG_MIN = 0.001
EDGE = 1.5 - math.sqrt(2.0)
MESH = pl.DeviceIdType.MESH
GAP = 40
ROWS = 88


def corner_bits(corner_id):
    return [corner_id >> 2 & 1, corner_id >> 1 & 1, corner_id & 1]


def stiffness_table():
    poisson = 0.3
    lame_first = poisson / ((1.0 + poisson) * (1.0 - 2.0 * poisson))
    lame_shear = 1.0 / (2.0 * (1.0 + poisson))
    elastic = np.zeros((6, 6))
    elastic[:3, :3] = lame_first
    for dim_index in range(3):
        elastic[dim_index, dim_index] += 2.0 * lame_shear
        elastic[3 + dim_index, 3 + dim_index] = lame_shear
    corners = np.array([corner_bits(corner_id) for corner_id in range(8)])
    gauss_points = [0.5 - 0.5 / math.sqrt(3.0), 0.5 + 0.5 / math.sqrt(3.0)]
    matrix_sum = np.zeros((24, 24))
    for gauss_x in gauss_points:
        for gauss_y in gauss_points:
            for gauss_z in gauss_points:
                location = np.array([gauss_x, gauss_y, gauss_z])
                shape_values = np.where(corners == 1, location, 1.0 - location)
                gradients = np.zeros((8, 3))
                for dim_index in range(3):
                    slope_sign = np.where(corners[:, dim_index] == 1, 1.0, -1.0)
                    others = (
                        shape_values[:, (dim_index + 1) % 3] * shape_values[:, (dim_index + 2) % 3]
                    )
                    gradients[:, dim_index] = slope_sign * others
                strain = np.zeros((6, 24))
                for dim_index in range(3):
                    strain[dim_index, 8 * dim_index : 8 * dim_index + 8] = gradients[:, dim_index]
                for shear_index, (dim_p, dim_q) in enumerate([(0, 1), (1, 2), (0, 2)]):
                    strain[3 + shear_index, 8 * dim_p : 8 * dim_p + 8] = gradients[:, dim_q]
                    strain[3 + shear_index, 8 * dim_q : 8 * dim_q + 8] = gradients[:, dim_p]
                matrix_sum = matrix_sum + 0.125 * strain.T @ elastic @ strain
    return matrix_sum


def prolong_table():
    matrix_set = np.zeros((8, 24, 24))
    for child_id in range(8):
        child_bits = corner_bits(child_id)
        for fine_node in range(8):
            fine_bits = corner_bits(fine_node)
            for coarse_node in range(8):
                coarse_bits = corner_bits(coarse_node)
                factor = 1.0
                for dim_index in range(3):
                    position = (child_bits[dim_index] + fine_bits[dim_index]) / 2.0
                    factor = factor * (position if coarse_bits[dim_index] == 1 else 1.0 - position)
                for component in range(3):
                    matrix_set[child_id, 8 * component + fine_node, 8 * component + coarse_node] = (
                        factor
                    )
    return matrix_set


def fine_table():
    prolong = prolong_table()
    stiffness = stiffness_table()
    table = np.zeros((24, 24, 4, 4, 4))
    for outer_id in range(8):
        outer_bits = corner_bits(outer_id)
        for inner_id in range(8):
            inner_bits = corner_bits(inner_id)
            inner = prolong[inner_id].T @ stiffness @ prolong[inner_id]
            spot = tuple(2 * o + i for o, i in zip(outer_bits, inner_bits))
            table[(slice(None), slice(None)) + spot] = prolong[outer_id].T @ inner @ prolong[outer_id]
    return table


def split_16(values):
    high = jnp.asarray(values, jnp.float32).astype(jnp.bfloat16)
    low = (jnp.asarray(values, jnp.float32) - high.astype(jnp.float32)).astype(jnp.bfloat16)
    return high, low


def stencil_table():
    fine = fine_table()
    table = np.zeros((3, ROWS, 8, 4, 4, 4))
    for comp_b in range(3):
        for comp_a in range(3):
            for corner_k in range(8):
                bits_k = corner_bits(corner_k)
                for corner_l in range(8):
                    bits_l = corner_bits(corner_l)
                    step = [l - k + 1 for l, k in zip(bits_l, bits_k)]
                    row = comp_a * 27 + step[0] * 9 + step[1] * 3 + step[2]
                    block = fine[8 * comp_a + corner_k, 8 * comp_b + corner_l]
                    table[comp_b, row, corner_k] += block.transpose(2, 0, 1)
    high, low = split_16(table.reshape(3 * ROWS, 512))
    return jnp.concatenate([high, low], axis=0)


def deal_table():
    table = np.zeros((128, 128), np.float32)
    for cz in range(4):
        for elem in range(32):
            table[4 * elem + cz, 32 * cz + elem] = 1.0
    return jnp.asarray(table, jnp.bfloat16)


def spread_table():
    table = np.zeros((2, 4, 32, 2, 4, 2, 64), np.float32)
    for half in range(2):
        for cz in range(4):
            for elem in range(32):
                for bz in range(2):
                    table[half, cz, elem, bz, cz, half, elem + bz] = 1.0
    return jnp.asarray(table.reshape(256, 1024), jnp.bfloat16)


def dot(left, right):
    return jnp.dot(left, right, preferred_element_type=jnp.float32)


def turn(value, shift, axis):
    shift = shift % value.shape[axis]
    return value if shift == 0 else pltpu.roll(value, shift, axis)


def kernel(
    count_x,
    count_y,
    dens,
    pas,
    load,
    table_far,
    deal_far,
    spread_far,
    phys,
    sol,
    halo,
    units,
    loads,
    nodes,
    whole,
    last,
    stencil,
    table,
    deal,
    spread,
    wide,
    near_sem,
    halo_out,
    halo_in,
    unit_out,
    unit_in,
    load_out,
    load_in,
    node_out,
    node_in,
    whole_out,
    whole_in,
):
    at_x = lax.axis_index("gx")
    at_y = lax.axis_index("gy")

    def there(step_x, step_y):
        return (
            (at_x + step_x >= 0)
            & (at_x + step_x < count_x)
            & (at_y + step_y >= 0)
            & (at_y + step_y < count_y)
        )

    def place(step_x, step_y):
        return (at_x + step_x, at_y + step_y)

    fetches = [
        pltpu.make_async_copy(far, near, near_sem.at[index])
        for index, (far, near) in enumerate(
            [(deal_far, deal), (spread_far, spread), (table_far, table)]
        )
    ]
    for fetch in fetches:
        fetch.start()

    halo[...] = jnp.zeros_like(halo)
    units[...] = jnp.zeros_like(units)
    loads[...] = jnp.zeros_like(loads)
    nodes[...] = jnp.zeros_like(nodes)
    wide[...] = jnp.zeros_like(wide)

    barrier = pltpu.get_barrier_semaphore()
    close = [(x, y) for x in range(-2, 3) for y in range(-1, 2) if (x, y) != (0, 0)]
    heard = count_y - 1
    for step_x, step_y in close:

        @pl.when(there(step_x, step_y))
        def _(step_x=step_x, step_y=step_y):
            pl.semaphore_signal(
                barrier, inc=1, device_id=place(step_x, step_y), device_id_type=MESH
            )

        if step_x != 0:
            heard = heard + jnp.where(there(step_x, step_y), 1, 0)

    def greet(other, carry):
        @pl.when((other < at_y - 1) | (other > at_y + 1))
        def _():
            pl.semaphore_signal(barrier, inc=1, device_id=(at_x, other), device_id_type=MESH)

        return carry

    lax.fori_loop(0, count_y, greet, 0)

    for row in range(24):
        by = row // 2 % 2
        wide[row, 2 + by : 6 + by, 0:32] = load[row, 0]
    for bx in range(2):
        total = None
        for comp in range(3):
            for bz in range(2):
                row = 8 * comp + 4 * bx + bz
                term = turn(wide[row] + wide[row + 2], GAP * comp + bz, 1)
                total = term if total is None else total + term
        loads[2, 1, bx] = total

    pl.semaphore_wait(barrier, heard)

    def halo_parts(step_x, step_y):
        source_x = pl.ds(0, 4) if step_x == 0 else pl.ds(3, 1) if step_x == 1 else pl.ds(0, 1)
        target_x = pl.ds(1, 4) if step_x == 0 else pl.ds(0, 1) if step_x == 1 else pl.ds(5, 1)
        source_y = pl.ds(0, 16) if step_y == 0 else pl.ds(8, 8) if step_y == 1 else pl.ds(0, 8)
        target_y = pl.ds(8, 16) if step_y == 0 else pl.ds(0, 8) if step_y == 1 else pl.ds(24, 8)
        return dens.at[source_x, source_y], halo.at[target_x, target_y]

    def unit_parts(step_x, step_y):
        rows, target = {0: ((2, 4), 2), 1: ((4, 2), 0), -1: ((2, 1), 6)}[step_y]
        return (
            units.at[2, pl.ds(rows[0], rows[1])],
            units.at[2 - step_x, pl.ds(target, rows[1])],
        )

    def load_parts(step_x, step_y):
        return loads.at[2, 1], loads.at[2 - step_x, 1 - step_y]

    def node_parts(turn_index):
        def parts(step_x, step_y):
            return nodes.at[turn_index, 2, 1], nodes.at[turn_index, 2 - step_x, 1 - step_y]

        return parts

    def exchange(steps, parts, out_sems, in_sems):
        def copy(index, step):
            source, target = parts(*step)
            return pltpu.make_async_remote_copy(
                source,
                target,
                out_sems.at[index],
                in_sems.at[index],
                device_id=place(*step),
                device_id_type=MESH,
            )

        def send():
            for index, step in enumerate(steps):

                @pl.when(there(*step))
                def _(index=index, step=step):
                    copy(index, step).start()

        def receive():
            for index, (step_x, step_y) in enumerate(steps):

                @pl.when(there(-step_x, -step_y))
                def _(index=index, step=(step_x, step_y)):
                    copy(index, step).wait_recv()

        def finish():
            for index, step in enumerate(steps):

                @pl.when(there(*step))
                def _(index=index, step=step):
                    copy(index, step).wait_send()

        return send, receive, finish

    ring = [(x, y) for x in range(-1, 2) for y in range(-1, 2) if (x, y) != (0, 0)]
    fan = [(x, y) for x in range(-1, 3) for y in range(-1, 2) if (x, y) != (0, 0)]
    halo_send, halo_receive, halo_finish = exchange(ring, halo_parts, halo_out, halo_in)
    load_send, load_receive, load_finish = exchange(fan, load_parts, load_out, load_in)
    unit_send, unit_receive, unit_finish = exchange(fan, unit_parts, unit_out, unit_in)
    halo_send()
    load_send()
    halo[1:5, 8:24] = dens[...]

    row_at = lax.broadcasted_iota(jnp.int32, (16, 128), 0) + 16 * at_y
    lane_at = lax.broadcasted_iota(jnp.int32, (16, 128), 1)
    near_y = 2.0 - jnp.where(row_at == 0, 1.0, 0.0) - jnp.where(row_at == 16 * count_y - 1, 1.0, 0.0)
    near_z = 2.0 - jnp.where(lane_at == 0, 1.0, 0.0) - jnp.where(lane_at == 127, 1.0, 0.0)
    lane_tall = lax.broadcasted_iota(jnp.int32, (32, 128), 1)
    halo_receive()
    beside, middle = [], []
    for layer in range(6):
        cells = halo[layer]
        along_z = jnp.where(lane_tall > 0, turn(cells, 1, 1), 0.0) + jnp.where(
            lane_tall < 127, turn(cells, -1, 1), 0.0
        )
        cross = along_z + turn(cells, 1, 0) + turn(cells, -1, 0)
        beside.append((0.5 * cells + EDGE * cross)[8:24])
        if 0 < layer < 5:
            corner = turn(along_z, 1, 0) + turn(along_z, -1, 0)
            middle.append((1.5 * cells + 0.5 * cross + EDGE * corner)[8:24])
    moduli = []
    for layer in range(4):
        place_x = 4 * at_x + layer
        near_x = (
            2.0
            - jnp.where(place_x == 0, 1.0, 0.0)
            - jnp.where(place_x == 4 * count_x - 1, 1.0, 0.0)
        )
        weight = (
            1.5
            + 0.5 * (near_x + near_y + near_z)
            + EDGE * (near_x * near_y + near_x * near_z + near_y * near_z)
        )
        filtered = (middle[layer] + beside[layer] + beside[layer + 2]) / weight
        solid = jnp.where(pas[layer] == 1, 1.0, filtered)
        phys[layer] = solid
        moduli.append(YOUNG_MIN + (1.0 - YOUNG_MIN) * (solid * solid * solid))

    fetches[0].wait()
    fine = jnp.concatenate(moduli, axis=0)
    high = fine.astype(jnp.bfloat16)
    low = (fine - high.astype(jnp.float32)).astype(jnp.bfloat16)
    dealt = dot(high, deal[...]) + dot(low, deal[...])
    upper = lax.broadcasted_iota(jnp.int32, (8, 128), 0) < 4
    for pair in range(2):
        for half in range(2):
            first = dealt[32 * pair + 8 * half : 32 * pair + 8 * half + 8]
            second = dealt[32 * pair + 16 + 8 * half : 32 * pair + 16 + 8 * half + 8]
            units[2, 2 + 2 * half, 8 * pair : 8 * pair + 8] = jnp.where(
                upper, first, turn(second, 4, 0)
            )
            units[2, 3 + 2 * half, 8 * pair : 8 * pair + 8] = jnp.where(
                upper, turn(first, 4, 0), second
            )
    unit_send()

    lane = lax.broadcasted_iota(jnp.int32, (8, 128), 1)
    row = lax.broadcasted_iota(jnp.int32, (8, 128), 0)
    group_0 = lane < GAP
    group_1 = lane < 2 * GAP
    last_row = jnp.where(at_y == count_y - 1, 6, 5)
    own = (row >= 2) & (row <= last_row)
    inner = (row >= 1) & (row <= 6)

    def window(left, centre, right):
        return jnp.where(row < 3, turn(left, 4, 0), 0.0) + centre + jnp.where(
            row > 5, turn(right, 4, 0), 0.0
        )

    load_receive()
    right_side = []
    for layer in range(1, 4):
        total = None
        for bx in range(2):
            term = window(*[loads[layer - bx, side, bx] for side in range(3)])
            total = term if total is None else total + term
        right_side.append(total)

    unit_receive()
    fetches[1].wait()
    fetches[2].wait()
    blank = jnp.zeros((16, 128), jnp.float32)
    spread_high, spread_low = [], []
    for layer in range(4):
        pieces = []
        for by in range(2):
            for pair in range(4):
                spots = [2 * pair - by, 2 * pair - by + 1]
                pieces.append(
                    jnp.concatenate(
                        [units[layer, q] if 0 <= q < 7 else blank for q in spots], axis=1
                    )
                )
        both = jnp.concatenate(pieces, axis=0)
        high = both.astype(jnp.bfloat16)
        low = (both - high.astype(jnp.float32)).astype(jnp.bfloat16)
        spread_high.append(dot(high, spread[...]).astype(jnp.bfloat16))
        spread_low.append(dot(low, spread[...]).astype(jnp.bfloat16))

    def around(parts, layer):
        rows = []
        for bx in range(2):
            for by in range(2):
                for bz in range(2):
                    for cz in range(4):
                        spot = 128 * (4 * bz + cz)
                        rows.append(
                            jnp.concatenate(
                                [
                                    parts[layer - bx][
                                        16 * (4 * by + pair) : 16 * (4 * by + pair) + 16,
                                        spot : spot + 128,
                                    ]
                                    for pair in range(4)
                                ],
                                axis=1,
                            )
                        )
        return jnp.concatenate(rows, axis=0)

    wide_lane = lax.broadcasted_iota(jnp.int32, (ROWS, 128), 1)
    table_high = table[0 : 3 * ROWS]
    table_low = table[3 * ROWS : 6 * ROWS]
    for layer in range(1, 4):
        high = around(spread_high, layer)
        low = around(spread_low, layer)
        terms = dot(table_high, high) + dot(table_high, low) + dot(table_low, high)
        for spot in range(1, 7):
            tiles = []
            for comp in range(3):
                tile = terms[
                    ROWS * comp : ROWS * comp + ROWS, 128 * (spot // 2) : 128 * (spot // 2) + 128
                ]
                tiles.append(turn(tile, GAP * comp - 64 * (spot % 2), 1))
            merged = jnp.where(
                wide_lane < GAP, tiles[0], jnp.where(wide_lane < 2 * GAP, tiles[1], tiles[2])
            )
            stencil[layer - 1, pl.ds(spot, ROWS, stride=8), :] = merged

    def entry(layer, index):
        return stencil[layer - 1, 8 * index : 8 * index + 8, :]

    def pick(parts):
        return jnp.where(group_0, parts[0], jnp.where(group_1, parts[1], parts[2]))

    scale = []
    for layer in range(1, 4):
        diagonal = pick([entry(layer, 27 * comp + 13) for comp in range(3)])
        real = inner & (diagonal > 0.0)
        if layer == 3:
            real = real & (at_x < count_x - 1)
        scale.append(jnp.where(real, RELAX / jnp.where(real, diagonal, 1.0), 0.0))

    def sweep(tiles, layer):
        sums = [None, None, None]
        for step_x in range(3):
            for step_z in range(3):
                moved_z = turn(tiles[layer + step_x - 1], 1 - step_z, 1)
                for step_y in range(3):
                    moved = turn(moved_z, 1 - step_y, 0)
                    for comp in range(3):
                        index = 27 * comp + 9 * step_x + 3 * step_y + step_z
                        term = entry(layer, index) * moved
                        sums[comp] = term if sums[comp] is None else sums[comp] + term
        product = pick(
            [
                sums[0] + turn(sums[0], -GAP, 1) + turn(sums[0], -2 * GAP, 1),
                sums[1] + turn(sums[1], GAP, 1) + turn(sums[1], -GAP, 1),
                sums[2] + turn(sums[2], GAP, 1) + turn(sums[2], 2 * GAP, 1),
            ]
        )
        factor = scale[layer - 1]
        updated = tiles[layer] + factor * (right_side[layer - 1] - product)
        return jnp.where(factor > 0.0, updated, 0.0)

    def first(layer):
        return jnp.where(scale[layer - 1] > 0.0, scale[layer - 1] * right_side[layer - 1], 0.0)

    tiles = {layer: first(layer) for layer in range(1, 4)}
    mine = jnp.where(own, sweep(tiles, 2), 0.0)
    finishes = [halo_finish, load_finish, unit_finish]
    for turn_index in range(2):
        nodes[turn_index, 2, 1] = mine
        node_send, node_receive, node_finish = exchange(
            close, node_parts(turn_index), node_out.at[turn_index], node_in.at[turn_index]
        )
        finishes.append(node_finish)
        node_send()
        node_receive()
        tiles = {}
        for layer in range(5):
            left, centre, right = [nodes[turn_index, layer, side] for side in range(3)]
            tiles[layer] = centre + (
                jnp.where(row < 2, turn(left, 4, 0), 0.0)
                + jnp.where(row > 5, turn(right, 4, 0), 0.0)
            )
        after = {layer: sweep(tiles, layer) for layer in range(1, 4)}
        mine = jnp.where(own, sweep(after, 2), 0.0)

    last[...] = mine
    whole[at_y] = mine

    def whole_copy(source, other):
        return pltpu.make_async_remote_copy(
            last,
            whole.at[source],
            whole_out.at[other],
            whole_in.at[source],
            device_id=(at_x, other),
            device_id_type=MESH,
        )

    def whole_send(other, carry):
        @pl.when(other != at_y)
        def _():
            whole_copy(at_y, other).start()

        return carry

    def whole_receive(other, carry):
        @pl.when(other != at_y)
        def _():
            whole_copy(other, other).wait_recv()

        return carry

    def whole_finish(other, carry):
        @pl.when(other != at_y)
        def _():
            whole_copy(at_y, other).wait_send()

        return carry

    lax.fori_loop(0, count_y, whole_send, 0)
    for finish in finishes:
        finish()
    lax.fori_loop(0, count_y, whole_receive, 0)
    for pair in range(count_y // 2):
        rows = jnp.where(upper, turn(whole[2 * pair], -2, 0), turn(whole[2 * pair + 1], 2, 0))
        for comp in range(3):
            sol[comp, 0, 8 * pair : 8 * pair + 8, :] = turn(rows, -GAP * comp, 1)[:, 0:33]
    for comp in range(3):
        sol[comp, 0, 4 * count_y : 4 * count_y + 1, :] = turn(
            whole[count_y - 1], -GAP * comp, 1
        )[6:7, 0:33]
    lax.fori_loop(0, count_y, whole_finish, 0)


def solution(mesh):
    count_x = mesh.shape["gx"]
    count_y = mesh.shape["gy"]

    def body(density, passive, element_load):
        vmem = pl.BlockSpec(memory_space=pltpu.VMEM)
        far = pl.BlockSpec(memory_space=pl.ANY)
        dma = pltpu.SemaphoreType.DMA

        def run(*operands):
            kernel(count_x, count_y, *operands)

        return pl.pallas_call(
            run,
            out_shape=(
                jax.ShapeDtypeStruct(density.shape, jnp.float32),
                jax.ShapeDtypeStruct((3, 1, 4 * count_y + 1, 33), jnp.float32),
            ),
            in_specs=[vmem, vmem, vmem, far, far, far],
            out_specs=(vmem, vmem),
            scratch_shapes=[
                pltpu.VMEM((6, 32, 128), jnp.float32),
                pltpu.VMEM((4, 7, 16, 128), jnp.float32),
                pltpu.VMEM((4, 3, 2, 8, 128), jnp.float32),
                pltpu.VMEM((2, 5, 3, 8, 128), jnp.float32),
                pltpu.VMEM((count_y, 8, 128), jnp.float32),
                pltpu.VMEM((8, 128), jnp.float32),
                pltpu.VMEM((3, 8 * ROWS, 128), jnp.float32),
                pltpu.VMEM((6 * ROWS, 512), jnp.bfloat16),
                pltpu.VMEM((128, 128), jnp.bfloat16),
                pltpu.VMEM((256, 1024), jnp.bfloat16),
                pltpu.VMEM((24, 8, 128), jnp.float32),
                dma((3,)),
                dma((8,)),
                dma((8,)),
                dma((11,)),
                dma((11,)),
                dma((11,)),
                dma((11,)),
                dma((2, 14)),
                dma((2, 14)),
                dma((count_y,)),
                dma((count_y,)),
            ],
            compiler_params=pltpu.CompilerParams(collective_id=0, has_side_effects=True),
        )(density, passive, element_load, stencil_table(), deal_table(), spread_table())

    return jax.shard_map(
        body,
        mesh=mesh,
        in_specs=(P("gx", "gy", None), P("gx", "gy", None), P(None, "gx", "gy", None)),
        out_specs=(P("gx", "gy", None), P(None, "gx", None, None)),
        check_vma=False,
    )
```

```python
import math

import jax
import jax.numpy as jnp
import numpy as np
from jax import lax
from jax.experimental import pallas as pl
from jax.experimental.pallas import tpu as pltpu
from jax.sharding import PartitionSpec as P

SWEEPS = 6
RELAX = 0.6
YOUNG_MIN = 0.001
EDGE = 1.5 - math.sqrt(2.0)
MESH = pl.DeviceIdType.MESH
GAP = 40
ROWS = 88
FULL = 272
CENTRE = 32


def corner_bits(corner_id):
    return [corner_id >> 2 & 1, corner_id >> 1 & 1, corner_id & 1]


def stiffness_table():
    poisson = 0.3
    lame_first = poisson / ((1.0 + poisson) * (1.0 - 2.0 * poisson))
    lame_shear = 1.0 / (2.0 * (1.0 + poisson))
    elastic = np.zeros((6, 6))
    elastic[:3, :3] = lame_first
    for dim_index in range(3):
        elastic[dim_index, dim_index] += 2.0 * lame_shear
        elastic[3 + dim_index, 3 + dim_index] = lame_shear
    corners = np.array([corner_bits(corner_id) for corner_id in range(8)])
    gauss_points = [0.5 - 0.5 / math.sqrt(3.0), 0.5 + 0.5 / math.sqrt(3.0)]
    matrix_sum = np.zeros((24, 24))
    for gauss_x in gauss_points:
        for gauss_y in gauss_points:
            for gauss_z in gauss_points:
                location = np.array([gauss_x, gauss_y, gauss_z])
                shape_values = np.where(corners == 1, location, 1.0 - location)
                gradients = np.zeros((8, 3))
                for dim_index in range(3):
                    slope_sign = np.where(corners[:, dim_index] == 1, 1.0, -1.0)
                    others = (
                        shape_values[:, (dim_index + 1) % 3] * shape_values[:, (dim_index + 2) % 3]
                    )
                    gradients[:, dim_index] = slope_sign * others
                strain = np.zeros((6, 24))
                for dim_index in range(3):
                    strain[dim_index, 8 * dim_index : 8 * dim_index + 8] = gradients[:, dim_index]
                for shear_index, (dim_p, dim_q) in enumerate([(0, 1), (1, 2), (0, 2)]):
                    strain[3 + shear_index, 8 * dim_p : 8 * dim_p + 8] = gradients[:, dim_q]
                    strain[3 + shear_index, 8 * dim_q : 8 * dim_q + 8] = gradients[:, dim_p]
                matrix_sum = matrix_sum + 0.125 * strain.T @ elastic @ strain
    return matrix_sum


def prolong_table():
    matrix_set = np.zeros((8, 24, 24))
    for child_id in range(8):
        child_bits = corner_bits(child_id)
        for fine_node in range(8):
            fine_bits = corner_bits(fine_node)
            for coarse_node in range(8):
                coarse_bits = corner_bits(coarse_node)
                factor = 1.0
                for dim_index in range(3):
                    position = (child_bits[dim_index] + fine_bits[dim_index]) / 2.0
                    factor = factor * (position if coarse_bits[dim_index] == 1 else 1.0 - position)
                for component in range(3):
                    matrix_set[child_id, 8 * component + fine_node, 8 * component + coarse_node] = (
                        factor
                    )
    return matrix_set


def fine_table():
    prolong = prolong_table()
    stiffness = stiffness_table()
    table = np.zeros((24, 24, 4, 4, 4))
    for outer_id in range(8):
        outer_bits = corner_bits(outer_id)
        for inner_id in range(8):
            inner_bits = corner_bits(inner_id)
            inner = prolong[inner_id].T @ stiffness @ prolong[inner_id]
            spot = tuple(2 * o + i for o, i in zip(outer_bits, inner_bits))
            table[(slice(None), slice(None)) + spot] = prolong[outer_id].T @ inner @ prolong[outer_id]
    return table


def split_16(values):
    high = jnp.asarray(values, jnp.float32).astype(jnp.bfloat16)
    low = (jnp.asarray(values, jnp.float32) - high.astype(jnp.float32)).astype(jnp.bfloat16)
    return high, low


def stencil_tables():
    fine = fine_table()
    table = np.zeros((3, ROWS, 8, 4, 4, 4))
    for comp_b in range(3):
        for comp_a in range(3):
            for corner_k in range(8):
                bits_k = corner_bits(corner_k)
                for corner_l in range(8):
                    bits_l = corner_bits(corner_l)
                    step = [l - k + 1 for l, k in zip(bits_l, bits_k)]
                    row = comp_a * 27 + step[0] * 9 + step[1] * 3 + step[2]
                    block = fine[8 * comp_a + corner_k, 8 * comp_b + corner_l]
                    table[comp_b, row, corner_k] += block.transpose(2, 0, 1)
    full = np.zeros((FULL, 512))
    full[: 3 * ROWS] = table.reshape(3 * ROWS, 512)
    centre = np.zeros((CENTRE, 512))
    for comp in range(3):
        centre[8 * comp : 8 * comp + 8] = table[comp, 27 * comp + 13].reshape(1, 512)
    return [jnp.concatenate(split_16(part), axis=0) for part in (full, centre)]


def deal_table():
    table = np.zeros((128, 128), np.float32)
    for cz in range(4):
        for elem in range(32):
            table[4 * elem + cz, 32 * cz + elem] = 1.0
    return jnp.asarray(table, jnp.bfloat16)


def spread_table():
    table = np.zeros((2, 4, 32, 2, 4, 2, 64), np.float32)
    for half in range(2):
        for cz in range(4):
            for elem in range(32):
                for bz in range(2):
                    table[half, cz, elem, bz, cz, half, elem + bz] = 1.0
    return jnp.asarray(table.reshape(256, 1024), jnp.bfloat16)


def dot(left, right):
    return jnp.dot(left, right, preferred_element_type=jnp.float32)


def turn(value, shift, axis):
    shift = shift % value.shape[axis]
    return value if shift == 0 else pltpu.roll(value, shift, axis)


def kernel(
    count_x,
    count_y,
    dens_far,
    pas_far,
    load_far,
    full_far,
    centre_far,
    deal_far,
    spread_far,
    phys_far,
    sol_far,
    phys,
    sol,
    halo,
    pas,
    load,
    units,
    loads,
    nodes,
    whole,
    last,
    stencil,
    full,
    centre,
    deal,
    spread,
    wide,
    near_sem,
    halo_out,
    halo_in,
    unit_out,
    unit_in,
    load_out,
    load_in,
    node_out,
    node_in,
    whole_sem,
):
    at_x = lax.axis_index("gx")
    at_y = lax.axis_index("gy")
    plane = at_x // 2
    half_x = at_x % 2
    planes = count_x // 2

    def beside_y(step_y):
        return lax.rem(at_y + (step_y + count_y), count_y)

    def guarded(condition, work):
        if condition is None:
            work()
        else:
            pl.when(condition)(work)

    def wait(ref, sem):
        pltpu.make_async_copy(ref, ref, sem).wait()

    def remote(source, target, out_sem, in_sem, to_x, to_y):
        return pltpu.make_async_remote_copy(
            source, target, out_sem, in_sem, device_id=(to_x, to_y), device_id_type=MESH
        )

    fetches = [
        pltpu.make_async_copy(far, near, near_sem.at[index])
        for index, (far, near) in enumerate(
            [
                (dens_far, halo.at[pl.ds(1, 4), pl.ds(8, 16)]),
                (pas_far, pas),
                (load_far, load),
                (deal_far, deal),
                (spread_far, spread),
                (full_far, full),
                (centre_far, centre),
            ]
        )
    ]
    for fetch in fetches:
        fetch.start()

    barrier = pltpu.get_barrier_semaphore()

    def greet(to_x, steps):
        for step in steps:
            pl.semaphore_signal(
                barrier, inc=1, device_id=(to_x, beside_y(step)), device_id_type=MESH
            )

    above = plane < planes - 1
    below = plane > 0
    greet(at_x, range(1, count_y))
    greet(2 * plane + 1 - half_x, (-1, 0, 1))
    for there, to in ((below, 2 * plane - 2), (above, 2 * plane + 2)):
        for side in range(2):
            guarded(there, lambda to=to, side=side: greet(to + side, (-1, 0, 1)))
    heard = count_y + 2 + jnp.where(below, 6, 0) + jnp.where(above, 6, 0)
    fetches[0].wait()
    pl.semaphore_wait(barrier, heard)

    before = at_x > 0
    after = at_x < count_x - 1
    source_y = {0: (8, 16), 1: (16, 8), -1: (8, 8)}
    target_y = {0: 8, 1: 0, -1: 24}

    def halo_send(step_x):
        source_x, target_x, deep = {0: (1, 1, 4), 1: (4, 0, 1), -1: (1, 5, 1)}[step_x]
        for step_y in (0, 1, -1):
            if step_x == 0 and step_y == 0:
                continue
            start, size = source_y[step_y]
            remote(
                halo.at[pl.ds(source_x, deep), pl.ds(start, size)],
                halo.at[pl.ds(target_x, deep), pl.ds(target_y[step_y], size)],
                halo_out.at[step_x + 1],
                halo_in.at[step_x + 1],
                at_x + step_x,
                beside_y(step_y),
            ).start()

    guarded(before, lambda: halo_send(-1))
    guarded(after, lambda: halo_send(1))
    halo_send(0)

    mine = 2 + half_x
    wide[...] = jnp.zeros_like(wide)
    fetches[2].wait()
    for row in range(24):
        by = row // 2 % 2
        wide[row, 2 + by : 6 + by, 0:32] = load[row, 0]
    for bx in range(2):
        total = None
        for comp in range(3):
            for bz in range(2):
                row = 8 * comp + 4 * bx + bz
                term = turn(wide[row] + wide[row + 2], GAP * comp + bz, 1)
                total = term if total is None else total + term
        loads[mine, 1, bx] = total

    targets = [
        (2 * plane + 2, half_x, 2 + half_x, 2, above),
        (2 * plane + 3, half_x, 2 + half_x, 3, above),
        (2 * plane - 2, 4, 4, 4, below & (half_x == 0)),
        (2 * plane - 1, 4, 4, 5, below & (half_x == 0)),
        (2 * plane + 1 - half_x, mine, 1, 1, None),
        (at_x, mine, 0, 0, None),
    ]

    def load_send(to_x, slot, in_index, out_index):
        for step_y in (0, 1, -1):
            if out_index == 0 and step_y == 0:
                continue
            remote(
                loads.at[mine, 1],
                loads.at[slot, 1 - step_y],
                load_out.at[out_index],
                load_in.at[in_index],
                to_x,
                beside_y(step_y),
            ).start()

    def unit_send(to_x, slot, in_index, out_index):
        for step_y in (0, 1, -1):
            if out_index == 0 and step_y == 0:
                continue
            start, target, size = {0: (2, 2, 4), 1: (4, 0, 2), -1: (2, 6, 1)}[step_y]
            remote(
                units.at[mine, pl.ds(start, size)],
                units.at[slot, pl.ds(target, size)],
                unit_out.at[out_index],
                unit_in.at[in_index],
                to_x,
                beside_y(step_y),
            ).start()

    for target in targets:
        guarded(target[4], lambda target=target: load_send(*target[:4]))

    row_at = lax.broadcasted_iota(jnp.int32, (16, 128), 0) + 16 * at_y
    lane_at = lax.broadcasted_iota(jnp.int32, (16, 128), 1)
    near_y = 2.0 - jnp.where(row_at == 0, 1.0, 0.0) - jnp.where(row_at == 16 * count_y - 1, 1.0, 0.0)
    near_z = 2.0 - jnp.where(lane_at == 0, 1.0, 0.0) - jnp.where(lane_at == 127, 1.0, 0.0)
    weights = []
    for layer in range(4):
        place_x = 4 * at_x + layer
        near_x = (
            2.0
            - jnp.where(place_x == 0, 1.0, 0.0)
            - jnp.where(place_x == 4 * count_x - 1, 1.0, 0.0)
        )
        weights.append(
            1.5
            + 0.5 * (near_x + near_y + near_z)
            + EDGE * (near_x * near_y + near_x * near_z + near_y * near_z)
        )
    lane_tall = lax.broadcasted_iota(jnp.int32, (32, 128), 1)
    row_tall = lax.broadcasted_iota(jnp.int32, (32, 128), 0) + (16 * at_y - 8)
    in_grid = (row_tall >= 0) & (row_tall < 16 * count_y)
    fetches[1].wait()
    fetches[3].wait()
    wait(halo.at[pl.ds(1, 4), pl.ds(0, 16)], halo_in.at[1])
    guarded(before, lambda: wait(halo.at[0], halo_in.at[2]))
    guarded(after, lambda: wait(halo.at[5], halo_in.at[0]))
    beside, middle = [], []
    for layer in range(6):
        inside = in_grid
        if layer == 0:
            inside = inside & before
        if layer == 5:
            inside = inside & after
        cells = jnp.where(inside, halo[layer], 0.0)
        along_z = jnp.where(lane_tall > 0, turn(cells, 1, 1), 0.0) + jnp.where(
            lane_tall < 127, turn(cells, -1, 1), 0.0
        )
        cross = along_z + turn(cells, 1, 0) + turn(cells, -1, 0)
        beside.append((0.5 * cells + EDGE * cross)[8:24])
        if 0 < layer < 5:
            corner = turn(along_z, 1, 0) + turn(along_z, -1, 0)
            middle.append((1.5 * cells + 0.5 * cross + EDGE * corner)[8:24])
    moduli = []
    for layer in range(4):
        filtered = (middle[layer] + beside[layer] + beside[layer + 2]) / weights[layer]
        solid = jnp.where(pas[layer] == 1, 1.0, filtered)
        phys[layer] = solid
        moduli.append(YOUNG_MIN + (1.0 - YOUNG_MIN) * (solid * solid * solid))

    fine = jnp.concatenate(moduli, axis=0)
    high = fine.astype(jnp.bfloat16)
    low = (fine - high.astype(jnp.float32)).astype(jnp.bfloat16)
    dealt = dot(jnp.concatenate([high, low], axis=0), deal[...])
    dealt = dealt[0:64] + dealt[64:128]
    upper = lax.broadcasted_iota(jnp.int32, (8, 128), 0) < 4
    for pair in range(2):
        for half in range(2):
            first = dealt[32 * pair + 8 * half : 32 * pair + 8 * half + 8]
            second = dealt[32 * pair + 16 + 8 * half : 32 * pair + 16 + 8 * half + 8]
            units[mine, 2 + 2 * half, 8 * pair : 8 * pair + 8] = jnp.where(
                upper, first, turn(second, 4, 0)
            )
            units[mine, 3 + 2 * half, 8 * pair : 8 * pair + 8] = jnp.where(
                upper, turn(first, 4, 0), second
            )
    for target in targets:
        guarded(target[4], lambda target=target: unit_send(*target[:4]))
    phys_copy = pltpu.make_async_copy(phys, phys_far, near_sem.at[7])
    phys_copy.start()

    lane = lax.broadcasted_iota(jnp.int32, (8, 128), 1)
    row = lax.broadcasted_iota(jnp.int32, (8, 128), 0)
    groups = [lane < GAP, (lane >= GAP) & (lane < 2 * GAP), lane >= 2 * GAP]
    last_row = jnp.where(at_y == count_y - 1, 6, 5)
    own = (row >= 2) & (row <= last_row)
    inner = (row >= 1) & (row <= 6)
    has_left = at_y > 0
    has_right = at_y < count_y - 1
    has_layer = [below, below, None, None, above, above]

    def kept(value, layer):
        return value if has_layer[layer] is None else jnp.where(has_layer[layer], value, 0.0)

    from_left = (row < 3) & has_left
    from_right = (row > 5) & has_right
    wait(loads.at[2, pl.ds(0, 2)], load_in.at[0])
    wait(loads.at[3], load_in.at[1])
    guarded(below, lambda: wait(loads.at[0], load_in.at[2]))
    guarded(below, lambda: wait(loads.at[1], load_in.at[3]))
    guarded(above, lambda: wait(loads.at[4], load_in.at[4]))
    right_side = []
    for layer in range(1, 5):
        total = None
        for bx in range(2):
            left, inside, right = [loads[layer - bx, side, bx] for side in range(3)]
            term = kept(
                jnp.where(from_left, turn(left, 4, 0), 0.0)
                + inside
                + jnp.where(from_right, turn(right, 4, 0), 0.0),
                layer - bx,
            )
            total = term if total is None else total + term
        right_side.append(total)

    def unit(layer, spot):
        value = units[layer, spot]
        if spot < 2:
            value = jnp.where(has_left, value, 0.0)
        if spot == 6:
            value = jnp.where(has_right, value, 0.0)
        return kept(value, layer)

    def around(layer):
        found = [unit(layer, spot) for spot in range(7)]
        pieces = []
        for by in range(2):
            for pair in range(3):
                spot = 2 * pair + 1 - by
                pieces.append(jnp.concatenate([found[spot], found[spot + 1]], axis=1))
        both = jnp.concatenate(pieces, axis=0)
        high = both.astype(jnp.bfloat16)
        low = (both - high.astype(jnp.float32)).astype(jnp.bfloat16)
        moved = dot(jnp.concatenate([high, low], axis=0), spread[...]).astype(jnp.bfloat16)
        results = []
        for part in range(2):
            rows = []
            for by in range(2):
                for bz in range(2):
                    for cz in range(4):
                        spot = 128 * (4 * bz + cz)
                        start = 96 * part + 48 * by
                        rows.append(
                            jnp.concatenate(
                                [
                                    moved[start + 16 * pair : start + 16 * pair + 16][
                                        :, spot : spot + 128
                                    ]
                                    for pair in range(3)
                                ],
                                axis=1,
                            )
                        )
            results.append(jnp.concatenate(rows, axis=0))
        return results

    def terms(table, bx, parts):
        count = table.shape[0] // 2
        both = dot(table[:, 256 * bx : 256 * bx + 256], parts[0])
        return (
            both[0:count]
            + both[count:]
            + dot(table[0:count, 256 * bx : 256 * bx + 256], parts[1])
        )

    wide_lane = lax.broadcasted_iota(jnp.int32, (ROWS, 128), 1)

    def build(layer, total):
        for spot in range(6):
            tiles = []
            for comp in range(3):
                tile = total[
                    ROWS * comp : ROWS * comp + ROWS, 128 * (spot // 2) : 128 * (spot // 2) + 128
                ]
                tiles.append(turn(tile, GAP * comp - 64 * (spot % 2), 1))
            merged = jnp.where(
                wide_lane < GAP, tiles[0], jnp.where(wide_lane < 2 * GAP, tiles[1], tiles[2])
            )
            stencil[layer - 1, pl.ds(spot + 1, ROWS, stride=8), :] = merged

    def scale_of(layer):
        total = terms(centre, 0, parts[layer]) + terms(centre, 1, parts[layer - 1])
        diagonal = jnp.zeros((8, 128), jnp.float32)
        for spot in range(6):
            for comp in range(3):
                tile = total[8 * comp : 8 * comp + 8, 128 * (spot // 2) : 128 * (spot // 2) + 128]
                tile = turn(tile, GAP * comp - 64 * (spot % 2), 1)
                diagonal = jnp.where((row == spot + 1) & groups[comp], tile, diagonal)
        real = inner & (diagonal > 0.0)
        if layer == 4:
            real = real & above
        return jnp.where(real, RELAX / jnp.where(real, diagonal, 1.0), 0.0)

    fetches[4].wait()
    fetches[5].wait()
    fetches[6].wait()
    parts = [None] * 5
    scale = [None] * 5
    wait(units.at[2, pl.ds(0, 3)], unit_in.at[0])
    wait(units.at[3], unit_in.at[1])
    parts[2] = around(2)
    parts[3] = around(3)
    build(3, terms(full, 0, parts[3]) + terms(full, 1, parts[2]))
    scale[3] = scale_of(3)
    guarded(below, lambda: wait(units.at[1], unit_in.at[3]))
    parts[1] = around(1)
    build(2, terms(full, 0, parts[2]) + terms(full, 1, parts[1]))
    scale[2] = scale_of(2)
    guarded(below, lambda: wait(units.at[0], unit_in.at[2]))
    parts[0] = around(0)
    scale[1] = scale_of(1)
    guarded(above, lambda: wait(units.at[4], unit_in.at[4]))
    parts[4] = around(4)
    scale[4] = scale_of(4)

    def entry(layer, index):
        return stencil[layer - 1, 8 * index : 8 * index + 8, :]

    def sweep(tiles, layer):
        sums = [None, None, None]
        for step_x in range(3):
            for step_z in range(3):
                moved_z = turn(tiles[layer + step_x - 1], 1 - step_z, 1)
                for step_y in range(3):
                    moved = turn(moved_z, 1 - step_y, 0)
                    for comp in range(3):
                        index = 27 * comp + 9 * step_x + 3 * step_y + step_z
                        term = entry(layer, index) * moved
                        sums[comp] = term if sums[comp] is None else sums[comp] + term
        product = jnp.where(
            groups[0],
            sums[0] + turn(sums[0], -GAP, 1) + turn(sums[0], -2 * GAP, 1),
            jnp.where(
                groups[1],
                sums[1] + turn(sums[1], GAP, 1) + turn(sums[1], -GAP, 1),
                sums[2] + turn(sums[2], GAP, 1) + turn(sums[2], 2 * GAP, 1),
            ),
        )
        factor = scale[layer]
        updated = tiles[layer] + factor * (right_side[layer - 1] - product)
        return jnp.where(factor > 0.0, updated, 0.0)

    def first(layer):
        return jnp.where(scale[layer] > 0.0, scale[layer] * right_side[layer - 1], 0.0)

    tiles = {layer: first(layer) for layer in range(1, 5)}
    pair_now = [jnp.where(own, sweep(tiles, layer), 0.0) for layer in (2, 3)]
    left_rows = (row < 2) & has_left
    right_rows = (row > 5) & has_right

    def node_send(turn_index, step_z):
        for step_y in (1, -1, 0):
            if step_z == 0 and step_y == 0:
                continue
            remote(
                nodes.at[turn_index, 1, pl.ds(2, 2)],
                nodes.at[turn_index, 1 - step_y, pl.ds(2 - 2 * step_z, 2)],
                node_out.at[turn_index, step_z + 1],
                node_in.at[turn_index, step_z + 1],
                at_x + 2 * step_z,
                beside_y(step_y),
            ).start()

    def node_wait(turn_index, sems, flip):
        up, down = (above, below) if flip else (below, above)
        wait(nodes.at[turn_index, 0, pl.ds(0, 4)], sems.at[turn_index, 1])
        guarded(up, lambda: wait(nodes.at[turn_index, 0], sems.at[turn_index, 2]))
        guarded(down, lambda: wait(nodes.at[turn_index, 0], sems.at[turn_index, 0]))

    for turn_index in range(2):
        nodes[turn_index, 1, 2] = pair_now[0]
        nodes[turn_index, 1, 3] = pair_now[1]
        guarded(above, lambda: node_send(turn_index, 1))
        guarded(below, lambda: node_send(turn_index, -1))
        node_send(turn_index, 0)
        if turn_index == 0:
            for layer in (1, 4):
                build(
                    layer,
                    terms(full, 0, parts[layer]) + terms(full, 1, parts[layer - 1]),
                )
        node_wait(turn_index, node_in, False)
        tiles = {}
        for layer in range(6):
            left, inside, right = [nodes[turn_index, side, layer] for side in range(3)]
            tiles[layer] = kept(
                jnp.where(
                    left_rows,
                    turn(left, 4, 0),
                    jnp.where(right_rows, turn(right, 4, 0), inside),
                ),
                layer,
            )
        later = {layer: sweep(tiles, layer) for layer in range(1, 5)}
        if turn_index == 0:
            pair_now = [jnp.where(own, sweep(later, layer), 0.0) for layer in (2, 3)]

    final = jnp.where(half_x == 0, sweep(later, 2), sweep(later, 3))
    final = jnp.where(own, final, 0.0)
    last[...] = final
    whole[at_y] = final
    for step in range(1, count_y):
        remote(last, whole.at[at_y], whole_sem.at[0], whole_sem.at[1], at_x, beside_y(step)).start()

    wait(halo.at[pl.ds(1, 4), pl.ds(0, 16)], halo_out.at[1])
    guarded(after, lambda: wait(halo.at[0], halo_out.at[2]))
    guarded(before, lambda: wait(halo.at[5], halo_out.at[0]))
    for to_x, slot, in_index, out_index, there in targets:
        some = pl.ds(0, 2) if out_index == 0 else pl.ds(0, 3)
        guarded(there, lambda: wait(loads.at[2, some], load_out.at[out_index]))
        some = pl.ds(0, 3) if out_index == 0 else pl.ds(0, 7)
        guarded(there, lambda: wait(units.at[2, some], unit_out.at[out_index]))
    for turn_index in range(2):
        node_wait(turn_index, node_out, True)
    phys_copy.wait()

    wait(whole.at[pl.ds(0, count_y - 1)], whole_sem.at[1])
    columns = []
    for pair in range(count_y // 2):
        columns.append(
            jnp.where(upper, turn(whole[2 * pair], -2, 0), turn(whole[2 * pair + 1], 2, 0))
        )
    columns.append(turn(whole[count_y - 1], -6, 0))
    columns.append(jnp.zeros((128 - 8 * len(columns), 128), jnp.float32))
    across = jnp.concatenate(columns, axis=0).T
    for comp in range(3):
        sol[comp, :, 0, :] = across[GAP * comp : GAP * comp + 33, 0 : 4 * count_y + 1]
    sol_copy = pltpu.make_async_copy(sol, sol_far, near_sem.at[8])
    sol_copy.start()
    wait(whole.at[pl.ds(0, count_y - 1)], whole_sem.at[0])
    sol_copy.wait()


def solution(mesh):
    count_x = mesh.shape["gx"]
    count_y = mesh.shape["gy"]

    def body(density, passive, element_load):
        far = pl.BlockSpec(memory_space=pl.ANY)
        dma = pltpu.SemaphoreType.DMA
        across_shape = (3, 33, 1, 4 * count_y + 1)

        def run(*refs):
            kernel(count_x, count_y, *refs)

        operands = [density, passive, element_load]
        operands += [*stencil_tables(), deal_table(), spread_table()]

        physical, across = pl.pallas_call(
            run,
            out_shape=(
                jax.ShapeDtypeStruct(density.shape, jnp.float32),
                jax.ShapeDtypeStruct(across_shape, jnp.float32),
            ),
            in_specs=[far] * 7,
            out_specs=(far, far),
            scratch_shapes=[
                pltpu.VMEM(density.shape, jnp.float32),
                pltpu.VMEM(across_shape, jnp.float32),
                pltpu.VMEM((6, 32, 128), jnp.float32),
                pltpu.VMEM(passive.shape, jnp.int32),
                pltpu.VMEM(element_load.shape, jnp.float32),
                pltpu.VMEM((5, 7, 16, 128), jnp.float32),
                pltpu.VMEM((5, 3, 2, 8, 128), jnp.float32),
                pltpu.VMEM((2, 3, 6, 8, 128), jnp.float32),
                pltpu.VMEM((count_y, 8, 128), jnp.float32),
                pltpu.VMEM((8, 128), jnp.float32),
                pltpu.VMEM((4, 8 * ROWS, 128), jnp.float32),
                pltpu.VMEM((2 * FULL, 512), jnp.bfloat16),
                pltpu.VMEM((2 * CENTRE, 512), jnp.bfloat16),
                pltpu.VMEM((128, 128), jnp.bfloat16),
                pltpu.VMEM((256, 1024), jnp.bfloat16),
                pltpu.VMEM((24, 8, 128), jnp.float32),
                dma((9,)),
                dma((3,)),
                dma((3,)),
                dma((6,)),
                dma((5,)),
                dma((6,)),
                dma((5,)),
                dma((2, 3)),
                dma((2, 3)),
                dma((2,)),
            ],
            compiler_params=pltpu.CompilerParams(collective_id=0, has_side_effects=True, vmem_limit_bytes=16 * 2**20),
        )(*[pltpu.with_memory_space_constraint(operand, pltpu.HBM) for operand in operands])
        return physical, across.transpose(0, 2, 3, 1)

    return jax.shard_map(
        body,
        mesh=mesh,
        in_specs=(P("gx", "gy", None), P("gx", "gy", None), P(None, "gx", "gy", None)),
        out_specs=(P("gx", "gy", None), P(None, "gx", None, None)),
        check_vma=False,
    )
```

```python
import math

import jax
import jax.numpy as jnp
import numpy as np
from jax import lax
from jax.experimental import pallas as pl
from jax.experimental.pallas import tpu as pltpu
from jax.sharding import PartitionSpec as P

SWEEPS = 6
RELAX = 0.6
YOUNG_MIN = 0.001
EDGE = 1.5 - math.sqrt(2.0)
MESH = pl.DeviceIdType.MESH
GAP = 40
ROWS = 88
FULL = 272
CENTRE = 32


def corner_bits(corner_id):
    return [corner_id >> 2 & 1, corner_id >> 1 & 1, corner_id & 1]


def stiffness_table():
    poisson = 0.3
    lame_first = poisson / ((1.0 + poisson) * (1.0 - 2.0 * poisson))
    lame_shear = 1.0 / (2.0 * (1.0 + poisson))
    elastic = np.zeros((6, 6))
    elastic[:3, :3] = lame_first
    for dim_index in range(3):
        elastic[dim_index, dim_index] += 2.0 * lame_shear
        elastic[3 + dim_index, 3 + dim_index] = lame_shear
    corners = np.array([corner_bits(corner_id) for corner_id in range(8)])
    gauss_points = [0.5 - 0.5 / math.sqrt(3.0), 0.5 + 0.5 / math.sqrt(3.0)]
    matrix_sum = np.zeros((24, 24))
    for gauss_x in gauss_points:
        for gauss_y in gauss_points:
            for gauss_z in gauss_points:
                location = np.array([gauss_x, gauss_y, gauss_z])
                shape_values = np.where(corners == 1, location, 1.0 - location)
                gradients = np.zeros((8, 3))
                for dim_index in range(3):
                    slope_sign = np.where(corners[:, dim_index] == 1, 1.0, -1.0)
                    others = (
                        shape_values[:, (dim_index + 1) % 3] * shape_values[:, (dim_index + 2) % 3]
                    )
                    gradients[:, dim_index] = slope_sign * others
                strain = np.zeros((6, 24))
                for dim_index in range(3):
                    strain[dim_index, 8 * dim_index : 8 * dim_index + 8] = gradients[:, dim_index]
                for shear_index, (dim_p, dim_q) in enumerate([(0, 1), (1, 2), (0, 2)]):
                    strain[3 + shear_index, 8 * dim_p : 8 * dim_p + 8] = gradients[:, dim_q]
                    strain[3 + shear_index, 8 * dim_q : 8 * dim_q + 8] = gradients[:, dim_p]
                matrix_sum = matrix_sum + 0.125 * strain.T @ elastic @ strain
    return matrix_sum


def prolong_table():
    matrix_set = np.zeros((8, 24, 24))
    for child_id in range(8):
        child_bits = corner_bits(child_id)
        for fine_node in range(8):
            fine_bits = corner_bits(fine_node)
            for coarse_node in range(8):
                coarse_bits = corner_bits(coarse_node)
                factor = 1.0
                for dim_index in range(3):
                    position = (child_bits[dim_index] + fine_bits[dim_index]) / 2.0
                    factor = factor * (position if coarse_bits[dim_index] == 1 else 1.0 - position)
                for component in range(3):
                    matrix_set[child_id, 8 * component + fine_node, 8 * component + coarse_node] = (
                        factor
                    )
    return matrix_set


def fine_table():
    prolong = prolong_table()
    stiffness = stiffness_table()
    table = np.zeros((24, 24, 4, 4, 4))
    for outer_id in range(8):
        outer_bits = corner_bits(outer_id)
        for inner_id in range(8):
            inner_bits = corner_bits(inner_id)
            inner = prolong[inner_id].T @ stiffness @ prolong[inner_id]
            spot = tuple(2 * o + i for o, i in zip(outer_bits, inner_bits))
            table[(slice(None), slice(None)) + spot] = prolong[outer_id].T @ inner @ prolong[outer_id]
    return table


def split_16(values):
    high = jnp.asarray(values, jnp.float32).astype(jnp.bfloat16)
    low = (jnp.asarray(values, jnp.float32) - high.astype(jnp.float32)).astype(jnp.bfloat16)
    return high, low


def stencil_tables():
    fine = fine_table()
    table = np.zeros((3, ROWS, 8, 4, 4, 4))
    for comp_b in range(3):
        for comp_a in range(3):
            for corner_k in range(8):
                bits_k = corner_bits(corner_k)
                for corner_l in range(8):
                    bits_l = corner_bits(corner_l)
                    step = [l - k + 1 for l, k in zip(bits_l, bits_k)]
                    row = comp_a * 27 + step[0] * 9 + step[1] * 3 + step[2]
                    block = fine[8 * comp_a + corner_k, 8 * comp_b + corner_l]
                    table[comp_b, row, corner_k] += block.transpose(2, 0, 1)
    full = np.zeros((FULL, 512))
    full[: 3 * ROWS] = table.reshape(3 * ROWS, 512)
    centre = np.zeros((CENTRE, 512))
    for comp in range(3):
        centre[8 * comp : 8 * comp + 8] = table[comp, 27 * comp + 13].reshape(1, 512)
    return [jnp.concatenate(split_16(part), axis=0) for part in (full, centre)]


def deal_table():
    table = np.zeros((128, 128), np.float32)
    for cz in range(4):
        for elem in range(32):
            table[4 * elem + cz, 32 * cz + elem] = 1.0
    return jnp.asarray(table, jnp.bfloat16)


def spread_table():
    table = np.zeros((2, 4, 32, 2, 4, 2, 64), np.float32)
    for half in range(2):
        for cz in range(4):
            for elem in range(32):
                for bz in range(2):
                    table[half, cz, elem, bz, cz, half, elem + bz] = 1.0
    return jnp.asarray(table.reshape(256, 1024), jnp.bfloat16)


def dot(left, right):
    return jnp.dot(left, right, preferred_element_type=jnp.float32)


def turn(value, shift, axis):
    shift = shift % value.shape[axis]
    return value if shift == 0 else pltpu.roll(value, shift, axis)


def kernel(
    count_x,
    count_y,
    dens_far,
    pas_far,
    load_far,
    full_far,
    centre_far,
    deal_far,
    spread_far,
    phys,
    sol,
    halo,
    pas,
    load,
    units,
    loads,
    nodes,
    whole,
    last,
    stencil,
    full,
    centre,
    deal,
    spread,
    wide,
    near_sem,
    halo_out,
    halo_in,
    unit_out,
    unit_in,
    load_out,
    load_in,
    node_out,
    node_in,
    whole_sem,
):
    at_x = lax.axis_index("gx")
    at_y = lax.axis_index("gy")
    plane = at_x // 2
    half_x = at_x % 2
    planes = count_x // 2

    def beside_y(step_y):
        return lax.rem(at_y + (step_y + count_y), count_y)

    def guarded(condition, work):
        if condition is None:
            work()
        else:
            pl.when(condition)(work)

    def wait(ref, sem):
        pltpu.make_async_copy(ref, ref, sem).wait()

    def remote(source, target, out_sem, in_sem, to_x, to_y):
        return pltpu.make_async_remote_copy(
            source, target, out_sem, in_sem, device_id=(to_x, to_y), device_id_type=MESH
        )

    fetches = [
        pltpu.make_async_copy(far, near, near_sem.at[index])
        for index, (far, near) in enumerate(
            [
                (dens_far, halo.at[pl.ds(1, 4), pl.ds(8, 16)]),
                (pas_far, pas),
                (load_far, load),
                (deal_far, deal),
                (spread_far, spread),
                (full_far, full),
                (centre_far, centre),
            ]
        )
    ]
    fetches[0].start()

    barrier = pltpu.get_barrier_semaphore()

    def greet(to_x, steps):
        for step in steps:
            pl.semaphore_signal(
                barrier, inc=1, device_id=(to_x, beside_y(step)), device_id_type=MESH
            )

    above = plane < planes - 1
    below = plane > 0
    for there, to in ((below, 2 * plane - 2), (above, 2 * plane + 2)):
        for side in range(2):
            guarded(there, lambda to=to, side=side: greet(to + side, (-1, 1, 0)))
    greet(2 * plane + 1 - half_x, (-1, 1, 0))
    far_first = sorted(
        range(1, count_y),
        key=lambda step: -(min(step // 2 % 4, 4 - step // 2 % 4) + step // 8 % 2),
    )
    greet(at_x, far_first)
    for fetch in fetches[1:]:
        fetch.start()
    heard = count_y + 2 + jnp.where(below, 6, 0) + jnp.where(above, 6, 0)
    fetches[0].wait()
    pl.semaphore_wait(barrier, heard)

    before = at_x > 0
    after = at_x < count_x - 1
    source_y = {0: (8, 16), 1: (16, 8), -1: (8, 8)}
    target_y = {0: 8, 1: 0, -1: 24}

    def halo_send(step_x):
        source_x, target_x, deep = {0: (1, 1, 4), 1: (4, 0, 1), -1: (1, 5, 1)}[step_x]
        for step_y in (0, 1, -1):
            if step_x == 0 and step_y == 0:
                continue
            start, size = source_y[step_y]
            remote(
                halo.at[pl.ds(source_x, deep), pl.ds(start, size)],
                halo.at[pl.ds(target_x, deep), pl.ds(target_y[step_y], size)],
                halo_out.at[step_x + 1],
                halo_in.at[step_x + 1],
                at_x + step_x,
                beside_y(step_y),
            ).start()

    guarded(before, lambda: halo_send(-1))
    guarded(after, lambda: halo_send(1))
    halo_send(0)

    mine = 2 + half_x
    wide[...] = jnp.zeros_like(wide)
    fetches[2].wait()
    for row in range(24):
        by = row // 2 % 2
        wide[row, 2 + by : 6 + by, 0:32] = load[row, 0]
    for bx in range(2):
        total = None
        for comp in range(3):
            for bz in range(2):
                row = 8 * comp + 4 * bx + bz
                term = turn(wide[row] + wide[row + 2], GAP * comp + bz, 1)
                total = term if total is None else total + term
        loads[mine, 1, bx] = total

    targets = [
        (2 * plane + 2, half_x, 2 + half_x, 2, above),
        (2 * plane + 3, half_x, 2 + half_x, 3, above),
        (2 * plane - 2, 4, 4, 4, below & (half_x == 0)),
        (2 * plane - 1, 4, 4, 5, below & (half_x == 0)),
        (2 * plane + 1 - half_x, mine, 1, 1, None),
        (at_x, mine, 0, 0, None),
    ]

    def load_send(to_x, slot, in_index, out_index):
        for step_y in (0, 1, -1):
            if out_index == 0 and step_y == 0:
                continue
            remote(
                loads.at[mine, 1],
                loads.at[slot, 1 - step_y],
                load_out.at[out_index],
                load_in.at[in_index],
                to_x,
                beside_y(step_y),
            ).start()

    def unit_send(to_x, slot, in_index, out_index):
        for step_y in (0, 1, -1):
            if out_index == 0 and step_y == 0:
                continue
            start, target, size = {0: (2, 2, 4), 1: (4, 0, 2), -1: (2, 6, 1)}[step_y]
            remote(
                units.at[mine, pl.ds(start, size)],
                units.at[slot, pl.ds(target, size)],
                unit_out.at[out_index],
                unit_in.at[in_index],
                to_x,
                beside_y(step_y),
            ).start()

    for target in targets:
        guarded(target[4], lambda target=target: load_send(*target[:4]))

    row_at = lax.broadcasted_iota(jnp.int32, (16, 128), 0) + 16 * at_y
    lane_at = lax.broadcasted_iota(jnp.int32, (16, 128), 1)
    near_y = 2.0 - jnp.where(row_at == 0, 1.0, 0.0) - jnp.where(row_at == 16 * count_y - 1, 1.0, 0.0)
    near_z = 2.0 - jnp.where(lane_at == 0, 1.0, 0.0) - jnp.where(lane_at == 127, 1.0, 0.0)
    weights = []
    for layer in range(4):
        place_x = 4 * at_x + layer
        near_x = (
            2.0
            - jnp.where(place_x == 0, 1.0, 0.0)
            - jnp.where(place_x == 4 * count_x - 1, 1.0, 0.0)
        )
        weights.append(
            1.5
            + 0.5 * (near_x + near_y + near_z)
            + EDGE * (near_x * near_y + near_x * near_z + near_y * near_z)
        )
    lane_tall = lax.broadcasted_iota(jnp.int32, (32, 128), 1)
    row_tall = lax.broadcasted_iota(jnp.int32, (32, 128), 0) + (16 * at_y - 8)
    in_grid = (row_tall >= 0) & (row_tall < 16 * count_y)
    fetches[1].wait()
    fetches[3].wait()
    wait(halo.at[pl.ds(1, 4), pl.ds(0, 16)], halo_in.at[1])
    guarded(before, lambda: wait(halo.at[0], halo_in.at[2]))
    guarded(after, lambda: wait(halo.at[5], halo_in.at[0]))
    beside, middle = [], []
    for layer in range(6):
        inside = in_grid
        if layer == 0:
            inside = inside & before
        if layer == 5:
            inside = inside & after
        cells = jnp.where(inside, halo[layer], 0.0)
        along_z = jnp.where(lane_tall > 0, turn(cells, 1, 1), 0.0) + jnp.where(
            lane_tall < 127, turn(cells, -1, 1), 0.0
        )
        cross = along_z + turn(cells, 1, 0) + turn(cells, -1, 0)
        beside.append((0.5 * cells + EDGE * cross)[8:24])
        if 0 < layer < 5:
            corner = turn(along_z, 1, 0) + turn(along_z, -1, 0)
            middle.append((1.5 * cells + 0.5 * cross + EDGE * corner)[8:24])
    moduli = []
    for layer in range(4):
        filtered = (middle[layer] + beside[layer] + beside[layer + 2]) / weights[layer]
        solid = jnp.where(pas[layer] == 1, 1.0, filtered)
        phys[layer] = solid
        moduli.append(YOUNG_MIN + (1.0 - YOUNG_MIN) * (solid * solid * solid))

    fine = jnp.concatenate(moduli, axis=0)
    high = fine.astype(jnp.bfloat16)
    low = (fine - high.astype(jnp.float32)).astype(jnp.bfloat16)
    dealt = dot(jnp.concatenate([high, low], axis=0), deal[...])
    dealt = dealt[0:64] + dealt[64:128]
    upper = lax.broadcasted_iota(jnp.int32, (8, 128), 0) < 4
    for pair in range(2):
        for half in range(2):
            first = dealt[32 * pair + 8 * half : 32 * pair + 8 * half + 8]
            second = dealt[32 * pair + 16 + 8 * half : 32 * pair + 16 + 8 * half + 8]
            units[mine, 2 + 2 * half, 8 * pair : 8 * pair + 8] = jnp.where(
                upper, first, turn(second, 4, 0)
            )
            units[mine, 3 + 2 * half, 8 * pair : 8 * pair + 8] = jnp.where(
                upper, turn(first, 4, 0), second
            )
    for target in targets:
        guarded(target[4], lambda target=target: unit_send(*target[:4]))

    lane = lax.broadcasted_iota(jnp.int32, (8, 128), 1)
    row = lax.broadcasted_iota(jnp.int32, (8, 128), 0)
    groups = [lane < GAP, (lane >= GAP) & (lane < 2 * GAP), lane >= 2 * GAP]
    last_row = jnp.where(at_y == count_y - 1, 6, 5)
    own = (row >= 2) & (row <= last_row)
    inner = (row >= 1) & (row <= 6)
    has_left = at_y > 0
    has_right = at_y < count_y - 1
    has_layer = [below, below, None, None, above, above]

    def kept(value, layer):
        return value if has_layer[layer] is None else jnp.where(has_layer[layer], value, 0.0)

    from_left = (row < 3) & has_left
    from_right = (row > 5) & has_right
    wait(loads.at[2, pl.ds(0, 2)], load_in.at[0])
    wait(loads.at[3], load_in.at[1])
    guarded(below, lambda: wait(loads.at[0], load_in.at[2]))
    guarded(below, lambda: wait(loads.at[1], load_in.at[3]))
    guarded(above, lambda: wait(loads.at[4], load_in.at[4]))
    right_side = []
    for layer in range(1, 5):
        total = None
        for bx in range(2):
            left, inside, right = [loads[layer - bx, side, bx] for side in range(3)]
            term = kept(
                jnp.where(from_left, turn(left, 4, 0), 0.0)
                + inside
                + jnp.where(from_right, turn(right, 4, 0), 0.0),
                layer - bx,
            )
            total = term if total is None else total + term
        right_side.append(total)

    def unit(layer, spot):
        value = units[layer, spot]
        if spot < 2:
            value = jnp.where(has_left, value, 0.0)
        if spot == 6:
            value = jnp.where(has_right, value, 0.0)
        return kept(value, layer)

    def around(layer):
        found = [unit(layer, spot) for spot in range(7)]
        pieces = []
        for by in range(2):
            for pair in range(3):
                spot = 2 * pair + 1 - by
                pieces.append(jnp.concatenate([found[spot], found[spot + 1]], axis=1))
        both = jnp.concatenate(pieces, axis=0)
        high = both.astype(jnp.bfloat16)
        low = (both - high.astype(jnp.float32)).astype(jnp.bfloat16)
        moved = dot(jnp.concatenate([high, low], axis=0), spread[...]).astype(jnp.bfloat16)
        results = []
        for part in range(2):
            rows = []
            for by in range(2):
                for bz in range(2):
                    for cz in range(4):
                        spot = 128 * (4 * bz + cz)
                        start = 96 * part + 48 * by
                        rows.append(
                            jnp.concatenate(
                                [
                                    moved[start + 16 * pair : start + 16 * pair + 16][
                                        :, spot : spot + 128
                                    ]
                                    for pair in range(3)
                                ],
                                axis=1,
                            )
                        )
            results.append(jnp.concatenate(rows, axis=0))
        return results

    def terms(table, bx, parts):
        count = table.shape[0] // 2
        both = dot(table[:, 256 * bx : 256 * bx + 256], parts[0])
        return (
            both[0:count]
            + both[count:]
            + dot(table[0:count, 256 * bx : 256 * bx + 256], parts[1])
        )

    wide_lane = lax.broadcasted_iota(jnp.int32, (ROWS, 128), 1)

    def build(layer, total):
        for spot in range(6):
            tiles = []
            for comp in range(3):
                tile = total[
                    ROWS * comp : ROWS * comp + ROWS, 128 * (spot // 2) : 128 * (spot // 2) + 128
                ]
                tiles.append(turn(tile, GAP * comp - 64 * (spot % 2), 1))
            merged = jnp.where(
                wide_lane < GAP, tiles[0], jnp.where(wide_lane < 2 * GAP, tiles[1], tiles[2])
            )
            stencil[layer - 1, pl.ds(spot + 1, ROWS, stride=8), :] = merged

    def scale_of(layer):
        total = terms(centre, 0, parts[layer]) + terms(centre, 1, parts[layer - 1])
        diagonal = jnp.zeros((8, 128), jnp.float32)
        for spot in range(6):
            for comp in range(3):
                tile = total[8 * comp : 8 * comp + 8, 128 * (spot // 2) : 128 * (spot // 2) + 128]
                tile = turn(tile, GAP * comp - 64 * (spot % 2), 1)
                diagonal = jnp.where((row == spot + 1) & groups[comp], tile, diagonal)
        real = inner & (diagonal > 0.0)
        if layer == 4:
            real = real & above
        return jnp.where(real, RELAX / jnp.where(real, diagonal, 1.0), 0.0)

    fetches[4].wait()
    fetches[5].wait()
    fetches[6].wait()
    parts = [None] * 5
    scale = [None] * 5
    wait(units.at[2, pl.ds(0, 3)], unit_in.at[0])
    wait(units.at[3], unit_in.at[1])
    parts[2] = around(2)
    parts[3] = around(3)
    build(3, terms(full, 0, parts[3]) + terms(full, 1, parts[2]))
    scale[3] = scale_of(3)
    guarded(below, lambda: wait(units.at[1], unit_in.at[3]))
    parts[1] = around(1)
    build(2, terms(full, 0, parts[2]) + terms(full, 1, parts[1]))
    scale[2] = scale_of(2)
    guarded(below, lambda: wait(units.at[0], unit_in.at[2]))
    parts[0] = around(0)
    scale[1] = scale_of(1)
    guarded(above, lambda: wait(units.at[4], unit_in.at[4]))
    parts[4] = around(4)
    scale[4] = scale_of(4)

    def entry(layer, index):
        return stencil[layer - 1, 8 * index : 8 * index + 8, :]

    def sweep(tiles, layer):
        sums = [None, None, None]
        for step_x in range(3):
            for step_z in range(3):
                moved_z = turn(tiles[layer + step_x - 1], 1 - step_z, 1)
                for step_y in range(3):
                    moved = turn(moved_z, 1 - step_y, 0)
                    for comp in range(3):
                        index = 27 * comp + 9 * step_x + 3 * step_y + step_z
                        term = entry(layer, index) * moved
                        sums[comp] = term if sums[comp] is None else sums[comp] + term
        product = jnp.where(
            groups[0],
            sums[0] + turn(sums[0], -GAP, 1) + turn(sums[0], -2 * GAP, 1),
            jnp.where(
                groups[1],
                sums[1] + turn(sums[1], GAP, 1) + turn(sums[1], -GAP, 1),
                sums[2] + turn(sums[2], GAP, 1) + turn(sums[2], 2 * GAP, 1),
            ),
        )
        factor = scale[layer]
        updated = tiles[layer] + factor * (right_side[layer - 1] - product)
        return jnp.where(factor > 0.0, updated, 0.0)

    def first(layer):
        return jnp.where(scale[layer] > 0.0, scale[layer] * right_side[layer - 1], 0.0)

    tiles = {layer: first(layer) for layer in range(1, 5)}
    pair_now = [jnp.where(own, sweep(tiles, layer), 0.0) for layer in (2, 3)]
    left_rows = (row < 2) & has_left
    right_rows = (row > 5) & has_right

    def node_send(turn_index, step_z):
        for step_y in (1, -1, 0):
            if step_z == 0 and step_y == 0:
                continue
            remote(
                nodes.at[turn_index, 1, pl.ds(2, 2)],
                nodes.at[turn_index, 1 - step_y, pl.ds(2 - 2 * step_z, 2)],
                node_out.at[turn_index, step_z + 1],
                node_in.at[turn_index, step_z + 1],
                at_x + 2 * step_z,
                beside_y(step_y),
            ).start()

    def node_wait(turn_index, sems, flip):
        up, down = (above, below) if flip else (below, above)
        wait(nodes.at[turn_index, 0, pl.ds(0, 4)], sems.at[turn_index, 1])
        guarded(up, lambda: wait(nodes.at[turn_index, 0], sems.at[turn_index, 2]))
        guarded(down, lambda: wait(nodes.at[turn_index, 0], sems.at[turn_index, 0]))

    for turn_index in range(2):
        nodes[turn_index, 1, 2] = pair_now[0]
        nodes[turn_index, 1, 3] = pair_now[1]
        guarded(above, lambda: node_send(turn_index, 1))
        guarded(below, lambda: node_send(turn_index, -1))
        node_send(turn_index, 0)
        if turn_index == 0:
            for layer in (1, 4):
                build(
                    layer,
                    terms(full, 0, parts[layer]) + terms(full, 1, parts[layer - 1]),
                )
        node_wait(turn_index, node_in, False)
        tiles = {}
        for layer in range(6):
            left, inside, right = [nodes[turn_index, side, layer] for side in range(3)]
            tiles[layer] = kept(
                jnp.where(
                    left_rows,
                    turn(left, 4, 0),
                    jnp.where(right_rows, turn(right, 4, 0), inside),
                ),
                layer,
            )
        later = {layer: sweep(tiles, layer) for layer in range(1, 5)}
        if turn_index == 0:
            pair_now = [jnp.where(own, sweep(later, layer), 0.0) for layer in (2, 3)]

    final = jnp.where(half_x == 0, sweep(later, 2), sweep(later, 3))
    final = jnp.where(own, final, 0.0)
    last[...] = final
    whole[at_y] = final
    for step in far_first:
        remote(last, whole.at[at_y], whole_sem.at[0], whole_sem.at[1], at_x, beside_y(step)).start()

    wait(halo.at[pl.ds(1, 4), pl.ds(0, 16)], halo_out.at[1])
    guarded(after, lambda: wait(halo.at[0], halo_out.at[2]))
    guarded(before, lambda: wait(halo.at[5], halo_out.at[0]))
    for to_x, slot, in_index, out_index, there in targets:
        some = pl.ds(0, 2) if out_index == 0 else pl.ds(0, 3)
        guarded(there, lambda: wait(loads.at[2, some], load_out.at[out_index]))
        some = pl.ds(0, 3) if out_index == 0 else pl.ds(0, 7)
        guarded(there, lambda: wait(units.at[2, some], unit_out.at[out_index]))
    for turn_index in range(2):
        node_wait(turn_index, node_out, True)

    wait(whole.at[pl.ds(0, count_y - 1)], whole_sem.at[1])
    columns = []
    for pair in range(count_y // 2):
        columns.append(
            jnp.where(upper, turn(whole[2 * pair], -2, 0), turn(whole[2 * pair + 1], 2, 0))
        )
    columns.append(turn(whole[count_y - 1], -6, 0))
    columns.append(jnp.zeros((128 - 8 * len(columns), 128), jnp.float32))
    across = jnp.concatenate(columns, axis=0).T
    for comp in range(3):
        sol[comp, :, 0, :] = across[GAP * comp : GAP * comp + 33, 0 : 4 * count_y + 1]
    wait(whole.at[pl.ds(0, count_y - 1)], whole_sem.at[0])


def solution(mesh):
    count_x = mesh.shape["gx"]
    count_y = mesh.shape["gy"]

    def body(density, passive, element_load):
        far = pl.BlockSpec(memory_space=pl.ANY)
        near = pl.BlockSpec(memory_space=pltpu.VMEM)
        dma = pltpu.SemaphoreType.DMA
        across_shape = (3, 33, 1, 4 * count_y + 1)

        def run(*refs):
            kernel(count_x, count_y, *refs)

        operands = [density, passive, element_load]
        operands += [*stencil_tables(), deal_table(), spread_table()]

        physical, across = pl.pallas_call(
            run,
            out_shape=(
                jax.ShapeDtypeStruct(density.shape, jnp.float32),
                jax.ShapeDtypeStruct(across_shape, jnp.float32),
            ),
            in_specs=[far] * 7,
            out_specs=(near, near),
            scratch_shapes=[
                pltpu.VMEM((6, 32, 128), jnp.float32),
                pltpu.VMEM(passive.shape, jnp.int32),
                pltpu.VMEM(element_load.shape, jnp.float32),
                pltpu.VMEM((5, 7, 16, 128), jnp.float32),
                pltpu.VMEM((5, 3, 2, 8, 128), jnp.float32),
                pltpu.VMEM((2, 3, 6, 8, 128), jnp.float32),
                pltpu.VMEM((count_y, 8, 128), jnp.float32),
                pltpu.VMEM((8, 128), jnp.float32),
                pltpu.VMEM((4, 8 * ROWS, 128), jnp.float32),
                pltpu.VMEM((2 * FULL, 512), jnp.bfloat16),
                pltpu.VMEM((2 * CENTRE, 512), jnp.bfloat16),
                pltpu.VMEM((128, 128), jnp.bfloat16),
                pltpu.VMEM((256, 1024), jnp.bfloat16),
                pltpu.VMEM((24, 8, 128), jnp.float32),
                dma((7,)),
                dma((3,)),
                dma((3,)),
                dma((6,)),
                dma((5,)),
                dma((6,)),
                dma((5,)),
                dma((2, 3)),
                dma((2, 3)),
                dma((2,)),
            ],
            compiler_params=pltpu.CompilerParams(collective_id=0, has_side_effects=True, vmem_limit_bytes=16 * 2**20),
        )(*[pltpu.with_memory_space_constraint(operand, pltpu.HBM) for operand in operands])
        def settle(physical_from, across_from, physical_to, across_to, sems):
            copies = [
                pltpu.make_async_copy(physical_from, physical_to, sems.at[0]),
                pltpu.make_async_copy(across_from, across_to, sems.at[1]),
            ]
            for copy in copies:
                copy.start()
            for copy in copies:
                copy.wait()

        physical, across = pl.pallas_call(
            settle,
            out_shape=(
                jax.ShapeDtypeStruct(density.shape, jnp.float32),
                jax.ShapeDtypeStruct(across_shape, jnp.float32),
            ),
            in_specs=[far, far],
            out_specs=(far, far),
            scratch_shapes=[dma((2,))],
            compiler_params=pltpu.CompilerParams(vmem_limit_bytes=2**20),
        )(physical, across)
        return physical, across.transpose(0, 2, 3, 1)

    return jax.shard_map(
        body,
        mesh=mesh,
        in_specs=(P("gx", "gy", None), P("gx", "gy", None), P(None, "gx", "gy", None)),
        out_specs=(P("gx", "gy", None), P(None, "gx", None, None)),
        check_vma=False,
    )
```

```python
import math

import jax
import jax.numpy as jnp
import numpy as np
from jax import lax
from jax.experimental import pallas as pl
from jax.experimental.pallas import tpu as pltpu
from jax.sharding import PartitionSpec as P

SWEEPS = 6
RELAX = 0.6
YOUNG_MIN = 0.001
EDGE = 1.5 - math.sqrt(2.0)
MESH = pl.DeviceIdType.MESH
GAP = 40
ROWS = 88
FULL = 272
CENTRE = 32


def corner_bits(corner_id):
    return [corner_id >> 2 & 1, corner_id >> 1 & 1, corner_id & 1]


def stiffness_table():
    poisson = 0.3
    lame_first = poisson / ((1.0 + poisson) * (1.0 - 2.0 * poisson))
    lame_shear = 1.0 / (2.0 * (1.0 + poisson))
    elastic = np.zeros((6, 6))
    elastic[:3, :3] = lame_first
    for dim_index in range(3):
        elastic[dim_index, dim_index] += 2.0 * lame_shear
        elastic[3 + dim_index, 3 + dim_index] = lame_shear
    corners = np.array([corner_bits(corner_id) for corner_id in range(8)])
    gauss_points = [0.5 - 0.5 / math.sqrt(3.0), 0.5 + 0.5 / math.sqrt(3.0)]
    matrix_sum = np.zeros((24, 24))
    for gauss_x in gauss_points:
        for gauss_y in gauss_points:
            for gauss_z in gauss_points:
                location = np.array([gauss_x, gauss_y, gauss_z])
                shape_values = np.where(corners == 1, location, 1.0 - location)
                gradients = np.zeros((8, 3))
                for dim_index in range(3):
                    slope_sign = np.where(corners[:, dim_index] == 1, 1.0, -1.0)
                    others = (
                        shape_values[:, (dim_index + 1) % 3] * shape_values[:, (dim_index + 2) % 3]
                    )
                    gradients[:, dim_index] = slope_sign * others
                strain = np.zeros((6, 24))
                for dim_index in range(3):
                    strain[dim_index, 8 * dim_index : 8 * dim_index + 8] = gradients[:, dim_index]
                for shear_index, (dim_p, dim_q) in enumerate([(0, 1), (1, 2), (0, 2)]):
                    strain[3 + shear_index, 8 * dim_p : 8 * dim_p + 8] = gradients[:, dim_q]
                    strain[3 + shear_index, 8 * dim_q : 8 * dim_q + 8] = gradients[:, dim_p]
                matrix_sum = matrix_sum + 0.125 * strain.T @ elastic @ strain
    return matrix_sum


def prolong_table():
    matrix_set = np.zeros((8, 24, 24))
    for child_id in range(8):
        child_bits = corner_bits(child_id)
        for fine_node in range(8):
            fine_bits = corner_bits(fine_node)
            for coarse_node in range(8):
                coarse_bits = corner_bits(coarse_node)
                factor = 1.0
                for dim_index in range(3):
                    position = (child_bits[dim_index] + fine_bits[dim_index]) / 2.0
                    factor = factor * (position if coarse_bits[dim_index] == 1 else 1.0 - position)
                for component in range(3):
                    matrix_set[child_id, 8 * component + fine_node, 8 * component + coarse_node] = (
                        factor
                    )
    return matrix_set


def fine_table():
    prolong = prolong_table()
    stiffness = stiffness_table()
    table = np.zeros((24, 24, 4, 4, 4))
    for outer_id in range(8):
        outer_bits = corner_bits(outer_id)
        for inner_id in range(8):
            inner_bits = corner_bits(inner_id)
            inner = prolong[inner_id].T @ stiffness @ prolong[inner_id]
            spot = tuple(2 * o + i for o, i in zip(outer_bits, inner_bits))
            table[(slice(None), slice(None)) + spot] = prolong[outer_id].T @ inner @ prolong[outer_id]
    return table


def split_16(values):
    high = jnp.asarray(values, jnp.float32).astype(jnp.bfloat16)
    low = (jnp.asarray(values, jnp.float32) - high.astype(jnp.float32)).astype(jnp.bfloat16)
    return high, low


def stencil_tables():
    fine = fine_table()
    table = np.zeros((3, ROWS, 8, 4, 4, 4))
    for comp_b in range(3):
        for comp_a in range(3):
            for corner_k in range(8):
                bits_k = corner_bits(corner_k)
                for corner_l in range(8):
                    bits_l = corner_bits(corner_l)
                    step = [l - k + 1 for l, k in zip(bits_l, bits_k)]
                    row = comp_a * 27 + step[0] * 9 + step[1] * 3 + step[2]
                    block = fine[8 * comp_a + corner_k, 8 * comp_b + corner_l]
                    table[comp_b, row, corner_k] += block.transpose(2, 0, 1)
    full = np.zeros((FULL, 512))
    full[: 3 * ROWS] = table.reshape(3 * ROWS, 512)
    centre = np.zeros((CENTRE, 512))
    for comp in range(3):
        centre[8 * comp : 8 * comp + 8] = table[comp, 27 * comp + 13].reshape(1, 512)
    return [jnp.concatenate(split_16(part), axis=0) for part in (full, centre)]


def deal_table():
    table = np.zeros((128, 128), np.float32)
    for cz in range(4):
        for elem in range(32):
            table[4 * elem + cz, 32 * cz + elem] = 1.0
    return jnp.asarray(table, jnp.bfloat16)


def spread_table():
    table = np.zeros((2, 4, 32, 2, 4, 2, 64), np.float32)
    for half in range(2):
        for cz in range(4):
            for elem in range(32):
                for bz in range(2):
                    table[half, cz, elem, bz, cz, half, elem + bz] = 1.0
    return jnp.asarray(table.reshape(256, 1024), jnp.bfloat16)


def dot(left, right):
    return jnp.dot(left, right, preferred_element_type=jnp.float32)


def turn(value, shift, axis):
    shift = shift % value.shape[axis]
    return value if shift == 0 else pltpu.roll(value, shift, axis)


def kernel(
    count_x,
    count_y,
    dens_far,
    pas_far,
    load_far,
    full_far,
    centre_far,
    deal_far,
    spread_far,
    phys,
    sol,
    halo,
    pas,
    load,
    units,
    loads,
    nodes,
    whole,
    last,
    stencil,
    full,
    centre,
    deal,
    spread,
    wide,
    near_sem,
    halo_out,
    halo_in,
    unit_out,
    unit_in,
    load_out,
    load_in,
    node_out,
    node_in,
    whole_sem,
):
    at_x = lax.axis_index("gx")
    at_y = lax.axis_index("gy")
    plane = at_x // 2
    half_x = at_x % 2
    planes = count_x // 2

    def beside_y(step_y):
        return lax.rem(at_y + (step_y + count_y), count_y)

    def guarded(condition, work):
        if condition is None:
            work()
        else:
            pl.when(condition)(work)

    def wait(ref, sem):
        pltpu.make_async_copy(ref, ref, sem).wait()

    def remote(source, target, out_sem, in_sem, to_x, to_y):
        return pltpu.make_async_remote_copy(
            source, target, out_sem, in_sem, device_id=(to_x, to_y), device_id_type=MESH
        )

    fetches = [
        pltpu.make_async_copy(far, near, near_sem.at[index])
        for index, (far, near) in enumerate(
            [
                (dens_far, halo.at[pl.ds(1, 4), pl.ds(8, 16)]),
                (pas_far, pas),
                (load_far, load),
                (deal_far, deal),
                (spread_far, spread),
                (full_far, full),
                (centre_far, centre),
            ]
        )
    ]
    fetches[0].start()

    barrier = pltpu.get_barrier_semaphore()

    def greet(to_x, steps):
        for step in steps:
            pl.semaphore_signal(
                barrier, inc=1, device_id=(to_x, beside_y(step)), device_id_type=MESH
            )

    above = plane < planes - 1
    below = plane > 0
    for there, to in ((below, 2 * plane - 2), (above, 2 * plane + 2)):
        for side in range(2):
            guarded(there, lambda to=to, side=side: greet(to + side, (-1, 1, 0)))
    greet(2 * plane + 1 - half_x, (-1, 1, 0))
    far_first = sorted(
        range(1, count_y),
        key=lambda step: -(min(step // 2 % 4, 4 - step // 2 % 4) + step // 8 % 2),
    )
    greet(at_x, far_first)
    for fetch in fetches[1:]:
        fetch.start()
    heard = count_y + 2 + jnp.where(below, 6, 0) + jnp.where(above, 6, 0)
    fetches[0].wait()
    pl.semaphore_wait(barrier, heard)

    before = at_x > 0
    after = at_x < count_x - 1
    source_y = {0: (8, 16), 1: (16, 8), -1: (8, 8)}
    target_y = {0: 8, 1: 0, -1: 24}

    def halo_send(step_x):
        source_x, target_x, deep = {0: (1, 1, 4), 1: (4, 0, 1), -1: (1, 5, 1)}[step_x]
        for step_y in (0, 1, -1):
            if step_x == 0 and step_y == 0:
                continue
            start, size = source_y[step_y]
            remote(
                halo.at[pl.ds(source_x, deep), pl.ds(start, size)],
                halo.at[pl.ds(target_x, deep), pl.ds(target_y[step_y], size)],
                halo_out.at[step_x + 1],
                halo_in.at[step_x + 1],
                at_x + step_x,
                beside_y(step_y),
            ).start()

    guarded(before, lambda: halo_send(-1))
    guarded(after, lambda: halo_send(1))
    halo_send(0)

    mine = 2 + half_x
    wide[...] = jnp.zeros_like(wide)
    fetches[2].wait()
    for row in range(24):
        by = row // 2 % 2
        wide[row, 2 + by : 6 + by, 0:32] = load[row, 0]
    for bx in range(2):
        total = None
        for comp in range(3):
            for bz in range(2):
                row = 8 * comp + 4 * bx + bz
                term = turn(wide[row] + wide[row + 2], GAP * comp + bz, 1)
                total = term if total is None else total + term
        loads[mine, 1, bx] = total

    targets = [
        (2 * plane + 2, half_x, 2 + half_x, 2, above),
        (2 * plane + 3, half_x, 2 + half_x, 3, above),
        (2 * plane - 2, 4, 4, 4, below & (half_x == 0)),
        (2 * plane - 1, 4, 4, 5, below & (half_x == 0)),
        (2 * plane + 1 - half_x, mine, 1, 1, None),
        (at_x, mine, 0, 0, None),
    ]

    def load_send(to_x, slot, in_index, out_index):
        for step_y in (0, 1, -1):
            if out_index == 0 and step_y == 0:
                continue
            remote(
                loads.at[mine, 1],
                loads.at[slot, 1 - step_y],
                load_out.at[out_index],
                load_in.at[in_index],
                to_x,
                beside_y(step_y),
            ).start()

    def unit_send(to_x, slot, in_index, out_index):
        for step_y in (0, 1, -1):
            if out_index == 0 and step_y == 0:
                continue
            start, target, size = {0: (2, 2, 4), 1: (4, 0, 2), -1: (2, 6, 1)}[step_y]
            remote(
                units.at[mine, pl.ds(start, size)],
                units.at[slot, pl.ds(target, size)],
                unit_out.at[out_index],
                unit_in.at[in_index],
                to_x,
                beside_y(step_y),
            ).start()

    for target in targets:
        guarded(target[4], lambda target=target: load_send(*target[:4]))

    row_at = lax.broadcasted_iota(jnp.int32, (16, 128), 0) + 16 * at_y
    lane_at = lax.broadcasted_iota(jnp.int32, (16, 128), 1)
    near_y = 2.0 - jnp.where(row_at == 0, 1.0, 0.0) - jnp.where(row_at == 16 * count_y - 1, 1.0, 0.0)
    near_z = 2.0 - jnp.where(lane_at == 0, 1.0, 0.0) - jnp.where(lane_at == 127, 1.0, 0.0)
    weights = []
    for layer in range(4):
        place_x = 4 * at_x + layer
        near_x = (
            2.0
            - jnp.where(place_x == 0, 1.0, 0.0)
            - jnp.where(place_x == 4 * count_x - 1, 1.0, 0.0)
        )
        weights.append(
            1.5
            + 0.5 * (near_x + near_y + near_z)
            + EDGE * (near_x * near_y + near_x * near_z + near_y * near_z)
        )
    lane_tall = lax.broadcasted_iota(jnp.int32, (32, 128), 1)
    row_tall = lax.broadcasted_iota(jnp.int32, (32, 128), 0) + (16 * at_y - 8)
    in_grid = (row_tall >= 0) & (row_tall < 16 * count_y)
    fetches[1].wait()
    fetches[3].wait()
    wait(halo.at[pl.ds(1, 4), pl.ds(0, 16)], halo_in.at[1])
    guarded(before, lambda: wait(halo.at[0], halo_in.at[2]))
    guarded(after, lambda: wait(halo.at[5], halo_in.at[0]))
    beside, middle = [], []
    for layer in range(6):
        inside = in_grid
        if layer == 0:
            inside = inside & before
        if layer == 5:
            inside = inside & after
        cells = jnp.where(inside, halo[layer], 0.0)
        along_z = jnp.where(lane_tall > 0, turn(cells, 1, 1), 0.0) + jnp.where(
            lane_tall < 127, turn(cells, -1, 1), 0.0
        )
        cross = along_z + turn(cells, 1, 0) + turn(cells, -1, 0)
        beside.append((0.5 * cells + EDGE * cross)[8:24])
        if 0 < layer < 5:
            corner = turn(along_z, 1, 0) + turn(along_z, -1, 0)
            middle.append((1.5 * cells + 0.5 * cross + EDGE * corner)[8:24])
    moduli = []
    for layer in range(4):
        filtered = (middle[layer] + beside[layer] + beside[layer + 2]) / weights[layer]
        solid = jnp.where(pas[layer] == 1, 1.0, filtered)
        phys[layer] = solid
        moduli.append(YOUNG_MIN + (1.0 - YOUNG_MIN) * (solid * solid * solid))

    fine = jnp.concatenate(moduli, axis=0)
    high = fine.astype(jnp.bfloat16)
    low = (fine - high.astype(jnp.float32)).astype(jnp.bfloat16)
    dealt = dot(jnp.concatenate([high, low], axis=0), deal[...])
    dealt = dealt[0:64] + dealt[64:128]
    upper = lax.broadcasted_iota(jnp.int32, (8, 128), 0) < 4
    for pair in range(2):
        for half in range(2):
            first = dealt[32 * pair + 8 * half : 32 * pair + 8 * half + 8]
            second = dealt[32 * pair + 16 + 8 * half : 32 * pair + 16 + 8 * half + 8]
            units[mine, 2 + 2 * half, 8 * pair : 8 * pair + 8] = jnp.where(
                upper, first, turn(second, 4, 0)
            )
            units[mine, 3 + 2 * half, 8 * pair : 8 * pair + 8] = jnp.where(
                upper, turn(first, 4, 0), second
            )
    for target in targets:
        guarded(target[4], lambda target=target: unit_send(*target[:4]))

    lane = lax.broadcasted_iota(jnp.int32, (8, 128), 1)
    row = lax.broadcasted_iota(jnp.int32, (8, 128), 0)
    groups = [lane < GAP, (lane >= GAP) & (lane < 2 * GAP), lane >= 2 * GAP]
    last_row = jnp.where(at_y == count_y - 1, 6, 5)
    own = (row >= 2) & (row <= last_row)
    inner = (row >= 1) & (row <= 6)
    has_left = at_y > 0
    has_right = at_y < count_y - 1
    has_layer = [below, below, None, None, above, above]

    def kept(value, layer):
        return value if has_layer[layer] is None else jnp.where(has_layer[layer], value, 0.0)

    from_left = (row < 3) & has_left
    from_right = (row > 5) & has_right
    wait(loads.at[2, pl.ds(0, 2)], load_in.at[0])
    wait(loads.at[3], load_in.at[1])
    guarded(below, lambda: wait(loads.at[0], load_in.at[2]))
    guarded(below, lambda: wait(loads.at[1], load_in.at[3]))
    guarded(above, lambda: wait(loads.at[4], load_in.at[4]))
    right_side = []
    for layer in range(1, 5):
        total = None
        for bx in range(2):
            left, inside, right = [loads[layer - bx, side, bx] for side in range(3)]
            term = kept(
                jnp.where(from_left, turn(left, 4, 0), 0.0)
                + inside
                + jnp.where(from_right, turn(right, 4, 0), 0.0),
                layer - bx,
            )
            total = term if total is None else total + term
        right_side.append(total)

    def unit(layer, spot):
        value = units[layer, spot]
        if spot < 2:
            value = jnp.where(has_left, value, 0.0)
        if spot == 6:
            value = jnp.where(has_right, value, 0.0)
        return kept(value, layer)

    def around(layer):
        found = [unit(layer, spot) for spot in range(7)]
        pieces = []
        for by in range(2):
            for pair in range(3):
                spot = 2 * pair + 1 - by
                pieces.append(jnp.concatenate([found[spot], found[spot + 1]], axis=1))
        both = jnp.concatenate(pieces, axis=0)
        high = both.astype(jnp.bfloat16)
        low = (both - high.astype(jnp.float32)).astype(jnp.bfloat16)
        moved = dot(jnp.concatenate([high, low], axis=0), spread[...]).astype(jnp.bfloat16)
        results = []
        for part in range(2):
            rows = []
            for by in range(2):
                for bz in range(2):
                    for cz in range(4):
                        spot = 128 * (4 * bz + cz)
                        start = 96 * part + 48 * by
                        rows.append(
                            jnp.concatenate(
                                [
                                    moved[start + 16 * pair : start + 16 * pair + 16][
                                        :, spot : spot + 128
                                    ]
                                    for pair in range(3)
                                ],
                                axis=1,
                            )
                        )
            results.append(jnp.concatenate(rows, axis=0))
        return results

    def terms(table, bx, parts):
        count = table.shape[0] // 2
        both = dot(table[:, 256 * bx : 256 * bx + 256], parts[0])
        return (
            both[0:count]
            + both[count:]
            + dot(table[0:count, 256 * bx : 256 * bx + 256], parts[1])
        )

    wide_lane = lax.broadcasted_iota(jnp.int32, (ROWS, 128), 1)

    def build(layer, total):
        for spot in range(6):
            tiles = []
            for comp in range(3):
                tile = total[
                    ROWS * comp : ROWS * comp + ROWS, 128 * (spot // 2) : 128 * (spot // 2) + 128
                ]
                tiles.append(turn(tile, GAP * comp - 64 * (spot % 2), 1))
            merged = jnp.where(
                wide_lane < GAP, tiles[0], jnp.where(wide_lane < 2 * GAP, tiles[1], tiles[2])
            )
            stencil[layer - 1, pl.ds(spot + 1, ROWS, stride=8), :] = merged

    def scale_of(layer):
        total = terms(centre, 0, parts[layer]) + terms(centre, 1, parts[layer - 1])
        diagonal = jnp.zeros((8, 128), jnp.float32)
        for spot in range(6):
            for comp in range(3):
                tile = total[8 * comp : 8 * comp + 8, 128 * (spot // 2) : 128 * (spot // 2) + 128]
                tile = turn(tile, GAP * comp - 64 * (spot % 2), 1)
                diagonal = jnp.where((row == spot + 1) & groups[comp], tile, diagonal)
        real = inner & (diagonal > 0.0)
        if layer == 4:
            real = real & above
        return jnp.where(real, RELAX / jnp.where(real, diagonal, 1.0), 0.0)

    fetches[4].wait()
    fetches[5].wait()
    fetches[6].wait()
    parts = [None] * 5
    scale = [None] * 5
    wait(units.at[2, pl.ds(0, 3)], unit_in.at[0])
    wait(units.at[3], unit_in.at[1])
    parts[2] = around(2)
    parts[3] = around(3)
    build(3, terms(full, 0, parts[3]) + terms(full, 1, parts[2]))
    scale[3] = scale_of(3)
    guarded(below, lambda: wait(units.at[1], unit_in.at[3]))
    guarded(below, lambda: wait(units.at[0], unit_in.at[2]))
    guarded(above, lambda: wait(units.at[4], unit_in.at[4]))
    for layer in (1, 0, 4):
        parts[layer] = around(layer)
    for layer in (1, 4, 2):
        scale[layer] = scale_of(layer)
    build(2, terms(full, 0, parts[2]) + terms(full, 1, parts[1]))

    def entry(layer, index):
        return stencil[layer - 1, 8 * index : 8 * index + 8, :]

    def sweep(tiles, layer):
        sums = [None, None, None]
        for step_x in range(3):
            for step_z in range(3):
                moved_z = turn(tiles[layer + step_x - 1], 1 - step_z, 1)
                for step_y in range(3):
                    moved = turn(moved_z, 1 - step_y, 0)
                    for comp in range(3):
                        index = 27 * comp + 9 * step_x + 3 * step_y + step_z
                        term = entry(layer, index) * moved
                        sums[comp] = term if sums[comp] is None else sums[comp] + term
        product = jnp.where(
            groups[0],
            sums[0] + turn(sums[0], -GAP, 1) + turn(sums[0], -2 * GAP, 1),
            jnp.where(
                groups[1],
                sums[1] + turn(sums[1], GAP, 1) + turn(sums[1], -GAP, 1),
                sums[2] + turn(sums[2], GAP, 1) + turn(sums[2], 2 * GAP, 1),
            ),
        )
        factor = scale[layer]
        updated = tiles[layer] + factor * (right_side[layer - 1] - product)
        return jnp.where(factor > 0.0, updated, 0.0)

    def first(layer):
        return jnp.where(scale[layer] > 0.0, scale[layer] * right_side[layer - 1], 0.0)

    tiles = {layer: first(layer) for layer in range(1, 5)}
    pair_now = [jnp.where(own, sweep(tiles, layer), 0.0) for layer in (2, 3)]
    left_rows = (row < 2) & has_left
    right_rows = (row > 5) & has_right

    def node_send(turn_index, step_z):
        for step_y in (1, -1, 0):
            if step_z == 0 and step_y == 0:
                continue
            remote(
                nodes.at[turn_index, 1, pl.ds(2, 2)],
                nodes.at[turn_index, 1 - step_y, pl.ds(2 - 2 * step_z, 2)],
                node_out.at[turn_index, step_z + 1],
                node_in.at[turn_index, step_z + 1],
                at_x + 2 * step_z,
                beside_y(step_y),
            ).start()

    def node_wait(turn_index, sems, flip):
        up, down = (above, below) if flip else (below, above)
        wait(nodes.at[turn_index, 0, pl.ds(0, 4)], sems.at[turn_index, 1])
        guarded(up, lambda: wait(nodes.at[turn_index, 0], sems.at[turn_index, 2]))
        guarded(down, lambda: wait(nodes.at[turn_index, 0], sems.at[turn_index, 0]))

    for turn_index in range(2):
        nodes[turn_index, 1, 2] = pair_now[0]
        nodes[turn_index, 1, 3] = pair_now[1]
        guarded(above, lambda: node_send(turn_index, 1))
        guarded(below, lambda: node_send(turn_index, -1))
        node_send(turn_index, 0)
        if turn_index == 0:
            for layer in (1, 4):
                build(
                    layer,
                    terms(full, 0, parts[layer]) + terms(full, 1, parts[layer - 1]),
                )
        node_wait(turn_index, node_in, False)
        tiles = {}
        for layer in range(6):
            left, inside, right = [nodes[turn_index, side, layer] for side in range(3)]
            tiles[layer] = kept(
                jnp.where(
                    left_rows,
                    turn(left, 4, 0),
                    jnp.where(right_rows, turn(right, 4, 0), inside),
                ),
                layer,
            )
        later = {layer: sweep(tiles, layer) for layer in range(1, 5)}
        if turn_index == 0:
            pair_now = [jnp.where(own, sweep(later, layer), 0.0) for layer in (2, 3)]

    final = jnp.where(half_x == 0, sweep(later, 2), sweep(later, 3))
    final = jnp.where(own, final, 0.0)
    last[...] = final
    whole[at_y] = final
    for step in far_first:
        remote(last, whole.at[at_y], whole_sem.at[0], whole_sem.at[1], at_x, beside_y(step)).start()

    wait(halo.at[pl.ds(1, 4), pl.ds(0, 16)], halo_out.at[1])
    guarded(after, lambda: wait(halo.at[0], halo_out.at[2]))
    guarded(before, lambda: wait(halo.at[5], halo_out.at[0]))
    for to_x, slot, in_index, out_index, there in targets:
        some = pl.ds(0, 2) if out_index == 0 else pl.ds(0, 3)
        guarded(there, lambda: wait(loads.at[2, some], load_out.at[out_index]))
        some = pl.ds(0, 3) if out_index == 0 else pl.ds(0, 7)
        guarded(there, lambda: wait(units.at[2, some], unit_out.at[out_index]))
    for turn_index in range(2):
        node_wait(turn_index, node_out, True)

    wait(whole.at[pl.ds(0, count_y - 1)], whole_sem.at[1])
    columns = []
    for pair in range(count_y // 2):
        columns.append(
            jnp.where(upper, turn(whole[2 * pair], -2, 0), turn(whole[2 * pair + 1], 2, 0))
        )
    columns.append(turn(whole[count_y - 1], -6, 0))
    columns.append(jnp.zeros((128 - 8 * len(columns), 128), jnp.float32))
    across = jnp.concatenate(columns, axis=0).T
    for comp in range(3):
        sol[comp, :, 0, :] = across[GAP * comp : GAP * comp + 33, 0 : 4 * count_y + 1]
    wait(whole.at[pl.ds(0, count_y - 1)], whole_sem.at[0])


def solution(mesh):
    count_x = mesh.shape["gx"]
    count_y = mesh.shape["gy"]

    def body(density, passive, element_load):
        far = pl.BlockSpec(memory_space=pl.ANY)
        near = pl.BlockSpec(memory_space=pltpu.VMEM)
        dma = pltpu.SemaphoreType.DMA
        across_shape = (3, 33, 1, 4 * count_y + 1)

        def run(*refs):
            kernel(count_x, count_y, *refs)

        operands = [density, passive, element_load]
        operands += [*stencil_tables(), deal_table(), spread_table()]

        physical, across = pl.pallas_call(
            run,
            out_shape=(
                jax.ShapeDtypeStruct(density.shape, jnp.float32),
                jax.ShapeDtypeStruct(across_shape, jnp.float32),
            ),
            in_specs=[far] * 7,
            out_specs=(near, near),
            scratch_shapes=[
                pltpu.VMEM((6, 32, 128), jnp.float32),
                pltpu.VMEM(passive.shape, jnp.int32),
                pltpu.VMEM(element_load.shape, jnp.float32),
                pltpu.VMEM((5, 7, 16, 128), jnp.float32),
                pltpu.VMEM((5, 3, 2, 8, 128), jnp.float32),
                pltpu.VMEM((2, 3, 6, 8, 128), jnp.float32),
                pltpu.VMEM((count_y, 8, 128), jnp.float32),
                pltpu.VMEM((8, 128), jnp.float32),
                pltpu.VMEM((4, 8 * ROWS, 128), jnp.float32),
                pltpu.VMEM((2 * FULL, 512), jnp.bfloat16),
                pltpu.VMEM((2 * CENTRE, 512), jnp.bfloat16),
                pltpu.VMEM((128, 128), jnp.bfloat16),
                pltpu.VMEM((256, 1024), jnp.bfloat16),
                pltpu.VMEM((24, 8, 128), jnp.float32),
                dma((7,)),
                dma((3,)),
                dma((3,)),
                dma((6,)),
                dma((5,)),
                dma((6,)),
                dma((5,)),
                dma((2, 3)),
                dma((2, 3)),
                dma((2,)),
            ],
            compiler_params=pltpu.CompilerParams(collective_id=0, has_side_effects=True, vmem_limit_bytes=16 * 2**20),
        )(*[pltpu.with_memory_space_constraint(operand, pltpu.HBM) for operand in operands])
        def settle(physical_from, across_from, physical_to, across_to, sems):
            copies = [
                pltpu.make_async_copy(physical_from, physical_to, sems.at[0]),
                pltpu.make_async_copy(across_from, across_to, sems.at[1]),
            ]
            for copy in copies:
                copy.start()
            for copy in copies:
                copy.wait()

        physical, across = pl.pallas_call(
            settle,
            out_shape=(
                jax.ShapeDtypeStruct(density.shape, jnp.float32),
                jax.ShapeDtypeStruct(across_shape, jnp.float32),
            ),
            in_specs=[far, far],
            out_specs=(far, far),
            scratch_shapes=[dma((2,))],
            compiler_params=pltpu.CompilerParams(vmem_limit_bytes=2**20),
        )(physical, across)
        return physical, across.transpose(0, 2, 3, 1)

    return jax.shard_map(
        body,
        mesh=mesh,
        in_specs=(P("gx", "gy", None), P("gx", "gy", None), P(None, "gx", "gy", None)),
        out_specs=(P("gx", "gy", None), P(None, "gx", None, None)),
        check_vma=False,
    )
```

```python
import math

import jax
import jax.numpy as jnp
import numpy as np
from jax import lax
from jax.experimental import pallas as pl
from jax.experimental.pallas import tpu as pltpu
from jax.sharding import PartitionSpec as P

SWEEPS = 6
RELAX = 0.6
YOUNG_MIN = 0.001
EDGE = 1.5 - math.sqrt(2.0)
MESH = pl.DeviceIdType.MESH
GAP = 40
ROWS = 88
FULL = 272
CENTRE = 32


def corner_bits(corner_id):
    return [corner_id >> 2 & 1, corner_id >> 1 & 1, corner_id & 1]


def stiffness_table():
    poisson = 0.3
    lame_first = poisson / ((1.0 + poisson) * (1.0 - 2.0 * poisson))
    lame_shear = 1.0 / (2.0 * (1.0 + poisson))
    elastic = np.zeros((6, 6))
    elastic[:3, :3] = lame_first
    for dim_index in range(3):
        elastic[dim_index, dim_index] += 2.0 * lame_shear
        elastic[3 + dim_index, 3 + dim_index] = lame_shear
    corners = np.array([corner_bits(corner_id) for corner_id in range(8)])
    gauss_points = [0.5 - 0.5 / math.sqrt(3.0), 0.5 + 0.5 / math.sqrt(3.0)]
    matrix_sum = np.zeros((24, 24))
    for gauss_x in gauss_points:
        for gauss_y in gauss_points:
            for gauss_z in gauss_points:
                location = np.array([gauss_x, gauss_y, gauss_z])
                shape_values = np.where(corners == 1, location, 1.0 - location)
                gradients = np.zeros((8, 3))
                for dim_index in range(3):
                    slope_sign = np.where(corners[:, dim_index] == 1, 1.0, -1.0)
                    others = (
                        shape_values[:, (dim_index + 1) % 3] * shape_values[:, (dim_index + 2) % 3]
                    )
                    gradients[:, dim_index] = slope_sign * others
                strain = np.zeros((6, 24))
                for dim_index in range(3):
                    strain[dim_index, 8 * dim_index : 8 * dim_index + 8] = gradients[:, dim_index]
                for shear_index, (dim_p, dim_q) in enumerate([(0, 1), (1, 2), (0, 2)]):
                    strain[3 + shear_index, 8 * dim_p : 8 * dim_p + 8] = gradients[:, dim_q]
                    strain[3 + shear_index, 8 * dim_q : 8 * dim_q + 8] = gradients[:, dim_p]
                matrix_sum = matrix_sum + 0.125 * strain.T @ elastic @ strain
    return matrix_sum


def prolong_table():
    matrix_set = np.zeros((8, 24, 24))
    for child_id in range(8):
        child_bits = corner_bits(child_id)
        for fine_node in range(8):
            fine_bits = corner_bits(fine_node)
            for coarse_node in range(8):
                coarse_bits = corner_bits(coarse_node)
                factor = 1.0
                for dim_index in range(3):
                    position = (child_bits[dim_index] + fine_bits[dim_index]) / 2.0
                    factor = factor * (position if coarse_bits[dim_index] == 1 else 1.0 - position)
                for component in range(3):
                    matrix_set[child_id, 8 * component + fine_node, 8 * component + coarse_node] = (
                        factor
                    )
    return matrix_set


def fine_table():
    prolong = prolong_table()
    stiffness = stiffness_table()
    table = np.zeros((24, 24, 4, 4, 4))
    for outer_id in range(8):
        outer_bits = corner_bits(outer_id)
        for inner_id in range(8):
            inner_bits = corner_bits(inner_id)
            inner = prolong[inner_id].T @ stiffness @ prolong[inner_id]
            spot = tuple(2 * o + i for o, i in zip(outer_bits, inner_bits))
            table[(slice(None), slice(None)) + spot] = prolong[outer_id].T @ inner @ prolong[outer_id]
    return table


def split_16(values):
    high = jnp.asarray(values, jnp.float32).astype(jnp.bfloat16)
    low = (jnp.asarray(values, jnp.float32) - high.astype(jnp.float32)).astype(jnp.bfloat16)
    return high, low


def stencil_tables():
    fine = fine_table()
    table = np.zeros((3, ROWS, 8, 4, 4, 4))
    for comp_b in range(3):
        for comp_a in range(3):
            for corner_k in range(8):
                bits_k = corner_bits(corner_k)
                for corner_l in range(8):
                    bits_l = corner_bits(corner_l)
                    step = [l - k + 1 for l, k in zip(bits_l, bits_k)]
                    row = comp_a * 27 + step[0] * 9 + step[1] * 3 + step[2]
                    block = fine[8 * comp_a + corner_k, 8 * comp_b + corner_l]
                    table[comp_b, row, corner_k] += block.transpose(2, 0, 1)
    full = np.zeros((FULL, 512))
    full[: 3 * ROWS] = table.reshape(3 * ROWS, 512)
    centre = np.zeros((CENTRE, 512))
    for comp in range(3):
        centre[8 * comp : 8 * comp + 8] = table[comp, 27 * comp + 13].reshape(1, 512)
    return [jnp.concatenate(split_16(part), axis=0) for part in (full, centre)]


def deal_table():
    table = np.zeros((128, 128), np.float32)
    for cz in range(4):
        for elem in range(32):
            table[4 * elem + cz, 32 * cz + elem] = 1.0
    return jnp.asarray(table, jnp.bfloat16)


def spread_table():
    table = np.zeros((2, 4, 32, 2, 4, 2, 64), np.float32)
    for half in range(2):
        for cz in range(4):
            for elem in range(32):
                for bz in range(2):
                    table[half, cz, elem, bz, cz, half, elem + bz] = 1.0
    return jnp.asarray(table.reshape(256, 1024), jnp.bfloat16)


def dot(left, right):
    return jnp.dot(left, right, preferred_element_type=jnp.float32)


def turn(value, shift, axis):
    shift = shift % value.shape[axis]
    return value if shift == 0 else pltpu.roll(value, shift, axis)


def kernel(
    count_x,
    count_y,
    dens_far,
    pas_far,
    load_far,
    full_far,
    centre_far,
    deal_far,
    spread_far,
    phys,
    sol,
    halo,
    pas,
    load,
    units,
    loads,
    nodes,
    whole,
    last,
    stencil,
    full,
    centre,
    deal,
    spread,
    wide,
    near_sem,
    halo_out,
    halo_in,
    unit_out,
    unit_in,
    load_out,
    load_in,
    node_out,
    node_in,
    whole_sem,
):
    at_x = lax.axis_index("gx")
    at_y = lax.axis_index("gy")
    plane = at_x // 2
    half_x = at_x % 2
    planes = count_x // 2

    def beside_y(step_y):
        return lax.rem(at_y + (step_y + count_y), count_y)

    def guarded(condition, work):
        if condition is None:
            work()
        else:
            pl.when(condition)(work)

    def wait(ref, sem):
        pltpu.make_async_copy(ref, ref, sem).wait()

    def remote(source, target, out_sem, in_sem, to_x, to_y):
        return pltpu.make_async_remote_copy(
            source, target, out_sem, in_sem, device_id=(to_x, to_y), device_id_type=MESH
        )

    fetches = [
        pltpu.make_async_copy(far, near, near_sem.at[index])
        for index, (far, near) in enumerate(
            [
                (dens_far, halo.at[pl.ds(1, 4), pl.ds(8, 16)]),
                (pas_far, pas),
                (load_far, load),
                (deal_far, deal),
                (spread_far, spread),
                (full_far, full),
                (centre_far, centre),
            ]
        )
    ]
    fetches[0].start()

    barrier = pltpu.get_barrier_semaphore()

    def greet(to_x, steps):
        for step in steps:
            pl.semaphore_signal(
                barrier, inc=1, device_id=(to_x, beside_y(step)), device_id_type=MESH
            )

    above = plane < planes - 1
    below = plane > 0
    for there, to in ((below, 2 * plane - 2), (above, 2 * plane + 2)):
        for side in range(2):
            guarded(there, lambda to=to, side=side: greet(to + side, (-1, 1, 0)))
    greet(2 * plane + 1 - half_x, (-1, 1, 0))
    far_first = sorted(
        range(1, count_y),
        key=lambda step: -(min(step // 2 % 4, 4 - step // 2 % 4) + step // 8 % 2),
    )
    greet(at_x, far_first)
    for fetch in fetches[1:]:
        fetch.start()
    heard = count_y + 2 + jnp.where(below, 6, 0) + jnp.where(above, 6, 0)
    fetches[0].wait()
    pl.semaphore_wait(barrier, heard)

    before = at_x > 0
    after = at_x < count_x - 1
    source_y = {0: (8, 16), 1: (16, 8), -1: (8, 8)}
    target_y = {0: 8, 1: 0, -1: 24}

    def halo_send(step_x):
        source_x, target_x, deep = {0: (1, 1, 4), 1: (4, 0, 1), -1: (1, 5, 1)}[step_x]
        for step_y in (0, 1, -1):
            if step_x == 0 and step_y == 0:
                continue
            start, size = source_y[step_y]
            remote(
                halo.at[pl.ds(source_x, deep), pl.ds(start, size)],
                halo.at[pl.ds(target_x, deep), pl.ds(target_y[step_y], size)],
                halo_out.at[step_x + 1],
                halo_in.at[step_x + 1],
                at_x + step_x,
                beside_y(step_y),
            ).start()

    guarded(before, lambda: halo_send(-1))
    guarded(after, lambda: halo_send(1))
    halo_send(0)

    mine = 2 + half_x
    wide[...] = jnp.zeros_like(wide)
    fetches[2].wait()
    for row in range(24):
        by = row // 2 % 2
        wide[row, 2 + by : 6 + by, 0:32] = load[row, 0]
    for bx in range(2):
        total = None
        for comp in range(3):
            for bz in range(2):
                row = 8 * comp + 4 * bx + bz
                term = turn(wide[row] + wide[row + 2], GAP * comp + bz, 1)
                total = term if total is None else total + term
        loads[mine, 1, bx] = total

    targets = [
        (2 * plane + 2, half_x, 2 + half_x, 2, above),
        (2 * plane + 3, half_x, 2 + half_x, 3, above),
        (2 * plane - 2, 4, 4, 4, below & (half_x == 0)),
        (2 * plane - 1, 4, 4, 5, below & (half_x == 0)),
        (2 * plane + 1 - half_x, mine, 1, 1, None),
        (at_x, mine, 0, 0, None),
    ]

    def load_send(to_x, slot, in_index, out_index):
        for step_y in (0, 1, -1):
            if out_index == 0 and step_y == 0:
                continue
            remote(
                loads.at[mine, 1],
                loads.at[slot, 1 - step_y],
                load_out.at[out_index],
                load_in.at[in_index],
                to_x,
                beside_y(step_y),
            ).start()

    def unit_send(to_x, slot, in_index, out_index):
        for step_y in (0, 1, -1):
            if out_index == 0 and step_y == 0:
                continue
            start, target, size = {0: (2, 2, 4), 1: (4, 0, 2), -1: (2, 6, 1)}[step_y]
            remote(
                units.at[mine, pl.ds(start, size)],
                units.at[slot, pl.ds(target, size)],
                unit_out.at[out_index],
                unit_in.at[in_index],
                to_x,
                beside_y(step_y),
            ).start()

    for target in targets:
        guarded(target[4], lambda target=target: load_send(*target[:4]))

    row_at = lax.broadcasted_iota(jnp.int32, (16, 128), 0) + 16 * at_y
    lane_at = lax.broadcasted_iota(jnp.int32, (16, 128), 1)
    near_y = 2.0 - jnp.where(row_at == 0, 1.0, 0.0) - jnp.where(row_at == 16 * count_y - 1, 1.0, 0.0)
    near_z = 2.0 - jnp.where(lane_at == 0, 1.0, 0.0) - jnp.where(lane_at == 127, 1.0, 0.0)
    weights = []
    for layer in range(4):
        place_x = 4 * at_x + layer
        near_x = (
            2.0
            - jnp.where(place_x == 0, 1.0, 0.0)
            - jnp.where(place_x == 4 * count_x - 1, 1.0, 0.0)
        )
        weights.append(
            1.5
            + 0.5 * (near_x + near_y + near_z)
            + EDGE * (near_x * near_y + near_x * near_z + near_y * near_z)
        )
    lane_tall = lax.broadcasted_iota(jnp.int32, (32, 128), 1)
    row_tall = lax.broadcasted_iota(jnp.int32, (32, 128), 0) + (16 * at_y - 8)
    in_grid = (row_tall >= 0) & (row_tall < 16 * count_y)
    fetches[1].wait()
    fetches[3].wait()
    wait(halo.at[pl.ds(1, 4), pl.ds(0, 16)], halo_in.at[1])
    guarded(before, lambda: wait(halo.at[0], halo_in.at[2]))
    guarded(after, lambda: wait(halo.at[5], halo_in.at[0]))
    beside, middle = [], []
    for layer in range(6):
        inside = in_grid
        if layer == 0:
            inside = inside & before
        if layer == 5:
            inside = inside & after
        cells = jnp.where(inside, halo[layer], 0.0)
        along_z = jnp.where(lane_tall > 0, turn(cells, 1, 1), 0.0) + jnp.where(
            lane_tall < 127, turn(cells, -1, 1), 0.0
        )
        cross = along_z + turn(cells, 1, 0) + turn(cells, -1, 0)
        beside.append((0.5 * cells + EDGE * cross)[8:24])
        if 0 < layer < 5:
            corner = turn(along_z, 1, 0) + turn(along_z, -1, 0)
            middle.append((1.5 * cells + 0.5 * cross + EDGE * corner)[8:24])
    moduli = []
    for layer in range(4):
        filtered = (middle[layer] + beside[layer] + beside[layer + 2]) / weights[layer]
        solid = jnp.where(pas[layer] == 1, 1.0, filtered)
        phys[layer] = solid
        moduli.append(YOUNG_MIN + (1.0 - YOUNG_MIN) * (solid * solid * solid))

    fine = jnp.concatenate(moduli, axis=0)
    high = fine.astype(jnp.bfloat16)
    low = (fine - high.astype(jnp.float32)).astype(jnp.bfloat16)
    dealt = dot(jnp.concatenate([high, low], axis=0), deal[...])
    dealt = dealt[0:64] + dealt[64:128]
    upper = lax.broadcasted_iota(jnp.int32, (8, 128), 0) < 4
    for pair in range(2):
        for half in range(2):
            first = dealt[32 * pair + 8 * half : 32 * pair + 8 * half + 8]
            second = dealt[32 * pair + 16 + 8 * half : 32 * pair + 16 + 8 * half + 8]
            units[mine, 2 + 2 * half, 8 * pair : 8 * pair + 8] = jnp.where(
                upper, first, turn(second, 4, 0)
            )
            units[mine, 3 + 2 * half, 8 * pair : 8 * pair + 8] = jnp.where(
                upper, turn(first, 4, 0), second
            )
    for target in targets:
        guarded(target[4], lambda target=target: unit_send(*target[:4]))

    lane = lax.broadcasted_iota(jnp.int32, (8, 128), 1)
    row = lax.broadcasted_iota(jnp.int32, (8, 128), 0)
    groups = [lane < GAP, (lane >= GAP) & (lane < 2 * GAP), lane >= 2 * GAP]
    last_row = jnp.where(at_y == count_y - 1, 6, 5)
    own = (row >= 2) & (row <= last_row)
    inner = (row >= 1) & (row <= 6)
    has_left = at_y > 0
    has_right = at_y < count_y - 1
    has_layer = [below, below, None, None, above, above]

    def kept(value, layer):
        return value if has_layer[layer] is None else jnp.where(has_layer[layer], value, 0.0)

    from_left = (row < 3) & has_left
    from_right = (row > 5) & has_right
    wait(loads.at[2, pl.ds(0, 2)], load_in.at[0])
    wait(loads.at[3], load_in.at[1])
    guarded(below, lambda: wait(loads.at[0], load_in.at[2]))
    guarded(below, lambda: wait(loads.at[1], load_in.at[3]))
    guarded(above, lambda: wait(loads.at[4], load_in.at[4]))
    right_side = []
    for layer in range(1, 5):
        total = None
        for bx in range(2):
            left, inside, right = [loads[layer - bx, side, bx] for side in range(3)]
            term = kept(
                jnp.where(from_left, turn(left, 4, 0), 0.0)
                + inside
                + jnp.where(from_right, turn(right, 4, 0), 0.0),
                layer - bx,
            )
            total = term if total is None else total + term
        right_side.append(total)

    def unit(layer, spot):
        value = units[layer, spot]
        if spot < 2:
            value = jnp.where(has_left, value, 0.0)
        if spot == 6:
            value = jnp.where(has_right, value, 0.0)
        return kept(value, layer)

    def around(layer):
        found = [unit(layer, spot) for spot in range(7)]
        pieces = []
        for by in range(2):
            for pair in range(3):
                spot = 2 * pair + 1 - by
                pieces.append(jnp.concatenate([found[spot], found[spot + 1]], axis=1))
        both = jnp.concatenate(pieces, axis=0)
        high = both.astype(jnp.bfloat16)
        low = (both - high.astype(jnp.float32)).astype(jnp.bfloat16)
        moved = dot(jnp.concatenate([high, low], axis=0), spread[...]).astype(jnp.bfloat16)
        results = []
        for part in range(2):
            rows = []
            for by in range(2):
                for bz in range(2):
                    for cz in range(4):
                        spot = 128 * (4 * bz + cz)
                        start = 96 * part + 48 * by
                        rows.append(
                            jnp.concatenate(
                                [
                                    moved[start + 16 * pair : start + 16 * pair + 16][
                                        :, spot : spot + 128
                                    ]
                                    for pair in range(3)
                                ],
                                axis=1,
                            )
                        )
            results.append(jnp.concatenate(rows, axis=0))
        return results

    def terms(table, bx, parts):
        count = table.shape[0] // 2
        both = dot(table[:, 256 * bx : 256 * bx + 256], parts[0])
        return (
            both[0:count]
            + both[count:]
            + dot(table[0:count, 256 * bx : 256 * bx + 256], parts[1])
        )

    wide_lane = lax.broadcasted_iota(jnp.int32, (ROWS, 128), 1)

    def build(layer, total):
        for spot in range(6):
            tiles = []
            for comp in range(3):
                tile = total[
                    ROWS * comp : ROWS * comp + ROWS, 128 * (spot // 2) : 128 * (spot // 2) + 128
                ]
                tiles.append(turn(tile, GAP * comp - 64 * (spot % 2), 1))
            merged = jnp.where(
                wide_lane < GAP, tiles[0], jnp.where(wide_lane < 2 * GAP, tiles[1], tiles[2])
            )
            stencil[layer - 1, pl.ds(spot + 1, ROWS, stride=8), :] = merged

    def scale_of(layer):
        total = terms(centre, 0, parts[layer]) + terms(centre, 1, parts[layer - 1])
        diagonal = jnp.zeros((8, 128), jnp.float32)
        for spot in range(6):
            for comp in range(3):
                tile = total[8 * comp : 8 * comp + 8, 128 * (spot // 2) : 128 * (spot // 2) + 128]
                tile = turn(tile, GAP * comp - 64 * (spot % 2), 1)
                diagonal = jnp.where((row == spot + 1) & groups[comp], tile, diagonal)
        real = inner & (diagonal > 0.0)
        if layer == 4:
            real = real & above
        return jnp.where(real, RELAX / jnp.where(real, diagonal, 1.0), 0.0)

    fetches[4].wait()
    fetches[5].wait()
    fetches[6].wait()
    parts = [None] * 5
    scale = [None] * 5
    wait(units.at[2, pl.ds(0, 3)], unit_in.at[0])
    wait(units.at[3], unit_in.at[1])
    parts[2] = around(2)
    parts[3] = around(3)
    build(3, terms(full, 0, parts[3]) + terms(full, 1, parts[2]))
    scale[3] = scale_of(3)
    half_2 = terms(full, 0, parts[2])
    guarded(below, lambda: wait(units.at[1], unit_in.at[3]))
    guarded(below, lambda: wait(units.at[0], unit_in.at[2]))
    guarded(above, lambda: wait(units.at[4], unit_in.at[4]))
    for layer in (1, 0, 4):
        parts[layer] = around(layer)
    own_2 = half_2 + terms(full, 1, parts[1])
    for layer in (1, 4, 2):
        scale[layer] = scale_of(layer)
    build(2, own_2)

    def entry(layer, index):
        return stencil[layer - 1, 8 * index : 8 * index + 8, :]

    def chosen(values, layer):
        return jnp.where(half_x == 0, values[layer], values[layer + 1])

    def sweep(tiles, layer, single=False):
        spot = layer + half_x if single else layer
        sums = [None, None, None]
        for step_x in range(3):
            for step_z in range(3):
                moved_z = turn(tiles[layer + step_x - 1], 1 - step_z, 1)
                for step_y in range(3):
                    moved = turn(moved_z, 1 - step_y, 0)
                    for comp in range(3):
                        index = 27 * comp + 9 * step_x + 3 * step_y + step_z
                        term = entry(spot, index) * moved
                        sums[comp] = term if sums[comp] is None else sums[comp] + term
        product = jnp.where(
            groups[0],
            sums[0] + turn(sums[0], -GAP, 1) + turn(sums[0], -2 * GAP, 1),
            jnp.where(
                groups[1],
                sums[1] + turn(sums[1], GAP, 1) + turn(sums[1], -GAP, 1),
                sums[2] + turn(sums[2], GAP, 1) + turn(sums[2], 2 * GAP, 1),
            ),
        )
        factor = chosen(scale, layer) if single else scale[layer]
        given = chosen(right_side, layer - 1) if single else right_side[layer - 1]
        updated = tiles[layer] + factor * (given - product)
        return jnp.where(factor > 0.0, updated, 0.0)

    def first(layer):
        return jnp.where(scale[layer] > 0.0, scale[layer] * right_side[layer - 1], 0.0)

    tiles = {layer: first(layer) for layer in range(1, 5)}
    pair_now = [jnp.where(own, sweep(tiles, layer), 0.0) for layer in (2, 3)]
    left_rows = (row < 2) & has_left
    right_rows = (row > 5) & has_right

    def node_send(turn_index, step_z):
        for step_y in (1, -1, 0):
            if step_z == 0 and step_y == 0:
                continue
            remote(
                nodes.at[turn_index, 1, pl.ds(2, 2)],
                nodes.at[turn_index, 1 - step_y, pl.ds(2 - 2 * step_z, 2)],
                node_out.at[turn_index, step_z + 1],
                node_in.at[turn_index, step_z + 1],
                at_x + 2 * step_z,
                beside_y(step_y),
            ).start()

    def node_wait(turn_index, sems, flip):
        up, down = (above, below) if flip else (below, above)
        wait(nodes.at[turn_index, 0, pl.ds(0, 4)], sems.at[turn_index, 1])
        guarded(up, lambda: wait(nodes.at[turn_index, 0], sems.at[turn_index, 2]))
        guarded(down, lambda: wait(nodes.at[turn_index, 0], sems.at[turn_index, 0]))

    for turn_index in range(2):
        nodes[turn_index, 1, 2] = pair_now[0]
        nodes[turn_index, 1, 3] = pair_now[1]
        guarded(above, lambda: node_send(turn_index, 1))
        guarded(below, lambda: node_send(turn_index, -1))
        node_send(turn_index, 0)
        if turn_index == 0:
            for layer in (1, 4):
                build(
                    layer,
                    terms(full, 0, parts[layer]) + terms(full, 1, parts[layer - 1]),
                )
        node_wait(turn_index, node_in, False)
        tiles = {}
        for layer in range(6):
            left, inside, right = [nodes[turn_index, side, layer] for side in range(3)]
            tiles[layer] = kept(
                jnp.where(
                    left_rows,
                    turn(left, 4, 0),
                    jnp.where(right_rows, turn(right, 4, 0), inside),
                ),
                layer,
            )
        if turn_index == 1:
            tiles = {layer: chosen(tiles, layer) for layer in range(5)}
            later = {layer: sweep(tiles, layer, True) for layer in range(1, 4)}
        else:
            later = {layer: sweep(tiles, layer) for layer in range(1, 5)}
            pair_now = [jnp.where(own, sweep(later, layer), 0.0) for layer in (2, 3)]

    final = jnp.where(own, sweep(later, 2, True), 0.0)
    last[...] = final
    whole[at_y] = final
    for step in far_first:
        remote(last, whole.at[at_y], whole_sem.at[0], whole_sem.at[1], at_x, beside_y(step)).start()

    wait(halo.at[pl.ds(1, 4), pl.ds(0, 16)], halo_out.at[1])
    guarded(after, lambda: wait(halo.at[0], halo_out.at[2]))
    guarded(before, lambda: wait(halo.at[5], halo_out.at[0]))
    for to_x, slot, in_index, out_index, there in targets:
        some = pl.ds(0, 2) if out_index == 0 else pl.ds(0, 3)
        guarded(there, lambda: wait(loads.at[2, some], load_out.at[out_index]))
        some = pl.ds(0, 3) if out_index == 0 else pl.ds(0, 7)
        guarded(there, lambda: wait(units.at[2, some], unit_out.at[out_index]))
    for turn_index in range(2):
        node_wait(turn_index, node_out, True)

    wait(whole.at[pl.ds(0, count_y - 1)], whole_sem.at[1])
    columns = []
    for pair in range(count_y // 2):
        columns.append(
            jnp.where(upper, turn(whole[2 * pair], -2, 0), turn(whole[2 * pair + 1], 2, 0))
        )
    columns.append(turn(whole[count_y - 1], -6, 0))
    columns.append(jnp.zeros((128 - 8 * len(columns), 128), jnp.float32))
    across = jnp.concatenate(columns, axis=0).T
    for comp in range(3):
        sol[comp, :, 0, :] = across[GAP * comp : GAP * comp + 33, 0 : 4 * count_y + 1]
    wait(whole.at[pl.ds(0, count_y - 1)], whole_sem.at[0])


def solution(mesh):
    count_x = mesh.shape["gx"]
    count_y = mesh.shape["gy"]

    def body(density, passive, element_load):
        far = pl.BlockSpec(memory_space=pl.ANY)
        near = pl.BlockSpec(memory_space=pltpu.VMEM)
        dma = pltpu.SemaphoreType.DMA
        across_shape = (3, 33, 1, 4 * count_y + 1)

        def run(*refs):
            kernel(count_x, count_y, *refs)

        operands = [density, passive, element_load]
        operands += [*stencil_tables(), deal_table(), spread_table()]

        physical, across = pl.pallas_call(
            run,
            out_shape=(
                jax.ShapeDtypeStruct(density.shape, jnp.float32),
                jax.ShapeDtypeStruct(across_shape, jnp.float32),
            ),
            in_specs=[far] * 7,
            out_specs=(near, near),
            scratch_shapes=[
                pltpu.VMEM((6, 32, 128), jnp.float32),
                pltpu.VMEM(passive.shape, jnp.int32),
                pltpu.VMEM(element_load.shape, jnp.float32),
                pltpu.VMEM((5, 7, 16, 128), jnp.float32),
                pltpu.VMEM((5, 3, 2, 8, 128), jnp.float32),
                pltpu.VMEM((2, 3, 6, 8, 128), jnp.float32),
                pltpu.VMEM((count_y, 8, 128), jnp.float32),
                pltpu.VMEM((8, 128), jnp.float32),
                pltpu.VMEM((4, 8 * ROWS, 128), jnp.float32),
                pltpu.VMEM((2 * FULL, 512), jnp.bfloat16),
                pltpu.VMEM((2 * CENTRE, 512), jnp.bfloat16),
                pltpu.VMEM((128, 128), jnp.bfloat16),
                pltpu.VMEM((256, 1024), jnp.bfloat16),
                pltpu.VMEM((24, 8, 128), jnp.float32),
                dma((7,)),
                dma((3,)),
                dma((3,)),
                dma((6,)),
                dma((5,)),
                dma((6,)),
                dma((5,)),
                dma((2, 3)),
                dma((2, 3)),
                dma((2,)),
            ],
            compiler_params=pltpu.CompilerParams(collective_id=0, has_side_effects=True, vmem_limit_bytes=16 * 2**20),
        )(*[pltpu.with_memory_space_constraint(operand, pltpu.HBM) for operand in operands])
        def settle(physical_from, across_from, physical_to, across_to, sems):
            copies = [
                pltpu.make_async_copy(physical_from, physical_to, sems.at[0]),
                pltpu.make_async_copy(across_from, across_to, sems.at[1]),
            ]
            for copy in copies:
                copy.start()
            for copy in copies:
                copy.wait()

        physical, across = pl.pallas_call(
            settle,
            out_shape=(
                jax.ShapeDtypeStruct(density.shape, jnp.float32),
                jax.ShapeDtypeStruct(across_shape, jnp.float32),
            ),
            in_specs=[far, far],
            out_specs=(far, far),
            scratch_shapes=[dma((2,))],
            compiler_params=pltpu.CompilerParams(vmem_limit_bytes=2**20),
        )(physical, across)
        return physical, across.transpose(0, 2, 3, 1)

    return jax.shard_map(
        body,
        mesh=mesh,
        in_specs=(P("gx", "gy", None), P("gx", "gy", None), P(None, "gx", "gy", None)),
        out_specs=(P("gx", "gy", None), P(None, "gx", None, None)),
        check_vma=False,
    )
```
